32 devices in a mesh: view: 4 (over z), cell: 8 (over y, x, core).
Axes of the slice: x: 2, y: 2, z: 4, core: 2. Of those that a mesh axis runs over, the one named last changes fastest.
Arguments:
- params: float32 [59, 65536], P(None, 'cell'), may hold values from -6.22 to 3.2, as said below
- camera: float32 [4, 11], P('view'), may hold values from -0.3 to 1536, as said below
- targets: float32 [4, 256, 3, 256], P('view', 'cell'), may hold values from 0 to 1
- send_blocks: int32 [4, 8, 8, 16], P('view', 'cell'), may hold values from 0 to 255, as said below
- tile_blocks: int32 [4, 256, 16], P('view', 'cell'), may hold values from -1 to 127, as said below
- tile_order: int32 [4, 256, 512], P('view', 'cell'), may hold values from 0 to 511, as said below
Outputs:
- image: float32 [4, 256, 3, 256], P('view', 'cell')
- grads: float32 [59, 65536], P(None, 'cell')
The draws below stay inside these ranges and needn't reach their ends.
Inputs may be any that keep to these rules, and one draw needn't show every extreme that they name: `params`: rows 0 to 2 lie in -3.2 to 3.2, rows 3 to 5 in log 0.002 to log 0.025, row 6 in 1 to 2, rows 7 to 9 in -1 to 1, row 10 in -3 to 2, rows 11 to 58 in -1.5 to 1.5. `camera`: quaternion first entry 1 to 2, its others -0.15 to 0.15, first two translation entries -0.3 to 0.3, third translation entry 4.5 to 6, focal lengths 2 to 3 times 16 max(32, 256 div 32), principal point within 20 of the image centre. `send_blocks`: the 16 numbers for one view, owner and receiving device are distinct. `tile_blocks`: A tile's live entries are distinct and come first, -1 fills the rest, and every tile has at least one live entry. `tile_order`: each tile's row is a permutation of 0 to 511.
All inputs are finite; a program needn't handle non-finite values.
Results may differ from the reference program's by a relative error of at most 0.0003.
Values sent between devices are 32-bit elements; how exact they have to be, the bound alone decides.
A program may use at most 128 MiB of HBM per device.

```python
import math
import jax
import jax.numpy as jnp
from jax import lax

BLOCK_GAUSSIANS = 32
PIX = 256
TX = 32
NB_DEV = 256
CAP = 16
TILE_LIST_BLOCKS = 16
TILES_PER_DEVICE = 32
CAMERA_VIEWS = 4
G_DEV = 8192
G = 65536
NT = 256
RECEIVED_SLOTS = 128
K = 512
N_CELL = 8


def quat_rows(quat):
    norm = jnp.sqrt(jnp.sum(quat * quat, axis=-1, keepdims=True))
    unit = quat / norm
    qw, qx, qy, qz = (unit[..., 0], unit[..., 1], unit[..., 2], unit[..., 3])
    rows = [[1.0 - 2.0 * (qy * qy + qz * qz), 2.0 * (qx * qy - qw * qz), 2.0 * (qx * qz + qw * qy)], [2.0 * (qx * qy + qw * qz), 1.0 - 2.0 * (qx * qx + qz * qz), 2.0 * (qy * qz - qw * qx)], [2.0 * (qx * qz - qw * qy), 2.0 * (qy * qz + qw * qx), 1.0 - 2.0 * (qx * qx + qy * qy)]]
    return rows


def make_camera(key):
    keys = jax.random.split(jax.random.fold_in(key, 21), 7)
    screen = 16.0 * max(TX, NT // TX)
    first = jax.random.uniform(keys[0], (CAMERA_VIEWS, 1), jnp.float32, 1.0, 2.0)
    others = jax.random.uniform(keys[1], (CAMERA_VIEWS, 3), jnp.float32, -0.15, 0.15)
    shift = jax.random.uniform(keys[2], (CAMERA_VIEWS, 2), jnp.float32, -0.3, 0.3)
    depth = jax.random.uniform(keys[3], (CAMERA_VIEWS, 1), jnp.float32, 4.5, 6.0)
    focal = screen * jax.random.uniform(keys[4], (CAMERA_VIEWS, 2), jnp.float32, 2.0, 3.0)
    centre_x = TX * 8.0 + jax.random.uniform(keys[5], (CAMERA_VIEWS, 1), jnp.float32, -20.0, 20.0)
    centre_y = NT // TX * 8.0 + jax.random.uniform(keys[6], (CAMERA_VIEWS, 1), jnp.float32, -20.0, 20.0)
    return jnp.concatenate([first, others, shift, depth, focal, centre_x, centre_y], axis=1)


def make_send_blocks(key):
    score_values = jax.random.randint(jax.random.fold_in(key, 31), (CAMERA_VIEWS, N_CELL, N_CELL, NB_DEV), 0, 4096)
    score_values = score_values * NB_DEV + jnp.arange(NB_DEV, dtype=jnp.int32)
    ranked = jnp.argsort(score_values, axis=-1, stable=True)
    return ranked[..., :CAP].astype(jnp.int32)


def make_tile_blocks(key):
    slot_sort_key = jax.random.fold_in(key, 41)
    count_key = jax.random.fold_in(key, 42)
    score_values = jax.random.randint(slot_sort_key, (CAMERA_VIEWS, N_CELL, RECEIVED_SLOTS), 0, 4096)
    score_values = score_values * RECEIVED_SLOTS + jnp.arange(RECEIVED_SLOTS, dtype=jnp.int32)
    shuffled = jnp.argsort(score_values, axis=-1, stable=True).astype(jnp.int32)
    local_part = jnp.arange(TILES_PER_DEVICE, dtype=jnp.int32)
    start_offsets = local_part * RECEIVED_SLOTS // TILES_PER_DEVICE
    window_span = (start_offsets[:, None] + jnp.arange(TILE_LIST_BLOCKS, dtype=jnp.int32)[None, :]) % RECEIVED_SLOTS
    picked = jnp.take(shuffled, window_span, axis=-1)
    counts = jax.random.randint(count_key, (CAMERA_VIEWS, N_CELL, TILES_PER_DEVICE, 1), max(1, TILE_LIST_BLOCKS // 2), TILE_LIST_BLOCKS + 1)
    counts = jnp.where(local_part[:, None] == 0, TILE_LIST_BLOCKS, counts)
    live = jnp.arange(TILE_LIST_BLOCKS, dtype=jnp.int32) < counts
    return jnp.where(live, picked, -1).reshape(CAMERA_VIEWS, NT, TILE_LIST_BLOCKS).astype(jnp.int32)


def make_tile_order(key):
    score_values = jax.random.randint(jax.random.fold_in(key, 51), (CAMERA_VIEWS, NT, K), 0, 4096)
    score_values = score_values * K + jnp.arange(K, dtype=jnp.int32)
    return jnp.argsort(score_values, axis=-1, stable=True).astype(jnp.int32)


def draw_camera(key, part):
    return make_camera(key)


def draw_send_blocks(key, part):
    return make_send_blocks(key)


def draw_tile_blocks(key, part):
    return make_tile_blocks(key)


def draw_tile_order(key, part):
    return make_tile_order(key)


def draw_params(key, part):
    keys = jax.random.split(jax.random.fold_in(key, 61), 11)
    camera = make_camera(key)
    sends = make_send_blocks(key)
    tiles = make_tile_blocks(key)
    order = make_tile_order(key)
    listed = CAMERA_VIEWS * NT * TILE_LIST_BLOCKS
    flat_slots = tiles.reshape(listed)
    live = flat_slots >= 0
    slot = jnp.maximum(flat_slots, 0)
    listing = jnp.arange(listed, dtype=jnp.int32)
    view_of = listing // (NT * TILE_LIST_BLOCKS)
    tile_of = listing // TILE_LIST_BLOCKS % NT
    dest = tile_of // TILES_PER_DEVICE
    source = slot // CAP
    column = slot % CAP
    local_block = sends[view_of, source, dest, column]
    blocks_all = NB_DEV * N_CELL
    owner_block = jnp.where(live, source * NB_DEV + local_block, blocks_all).astype(jnp.int32)
    ranked = jnp.argsort(owner_block, stable=True).astype(jnp.int32)
    counts = jax.ops.segment_sum(jnp.ones((listed,), jnp.int32), owner_block, num_segments=blocks_all + 1)[:blocks_all]
    start_offsets = jnp.cumsum(counts) - counts
    gauss = jnp.arange(G, dtype=jnp.int32)
    block_id = gauss // BLOCK_GAUSSIANS
    inner_product = gauss % BLOCK_GAUSSIANS
    count_here = counts[block_id]
    has_home = count_here > 0
    pick = ranked[jnp.minimum(start_offsets[block_id] + inner_product % jnp.maximum(count_here, 1), listed - 1)]
    inverse = jnp.argsort(order, axis=-1, stable=True).astype(jnp.int32)
    spare_view = jax.random.randint(keys[0], (G,), 0, CAMERA_VIEWS)
    spare_tile = jax.random.randint(keys[1], (G,), 0, NT)
    spare_rank = jax.random.randint(keys[2], (G,), 0, K)
    entry = pick % TILE_LIST_BLOCKS * BLOCK_GAUSSIANS + inner_product
    home_view = jnp.where(has_home, view_of[pick], spare_view)
    home_tile = jnp.where(has_home, tile_of[pick], spare_tile)
    rank = jnp.where(has_home, inverse[view_of[pick], tile_of[pick], entry], spare_rank)
    pix_x = (home_tile % TX * 16).astype(jnp.float32) + jax.random.uniform(keys[3], (G,), jnp.float32, -2.0, 18.0)
    pix_y = (home_tile // TX * 16).astype(jnp.float32) + jax.random.uniform(keys[4], (G,), jnp.float32, -2.0, 18.0)
    cam = camera[home_view]
    depth = cam[:, 6] - 0.5 + (rank.astype(jnp.float32) + jax.random.uniform(keys[5], (G,), jnp.float32, 0.0, 1.0)) / K
    rel = [(pix_x - cam[:, 9]) * depth / cam[:, 7] - cam[:, 4], (pix_y - cam[:, 10]) * depth / cam[:, 8] - cam[:, 5], depth - cam[:, 6]]
    rows = quat_rows(cam[:, 0:4])
    means = jnp.stack([rows[0][j] * rel[0] + rows[1][j] * rel[1] + rows[2][j] * rel[2] for j in range(3)])
    spread = jax.random.uniform(keys[6], (3, G), jnp.float32, 0.0, 1.0)
    colour = jnp.clip(0.5 * jax.random.normal(keys[7], (48, G), jnp.float32), -1.5, 1.5)
    log_scale = jnp.log(0.002) + jnp.log(12.5) * spread
    first = jax.random.uniform(keys[8], (1, G), jnp.float32, 1.0, 2.0)
    others = jax.random.uniform(keys[9], (3, G), jnp.float32, -1.0, 1.0)
    logit = jax.random.uniform(keys[10], (1, G), jnp.float32, -3.0, 2.0)
    return jnp.concatenate([means, log_scale, first, others, logit, colour], axis=0).astype(jnp.float32)


def block_scale(rng, shape, shards, least, top_value):
    def one(dim, shards_of):
        heights = jax.random.uniform(jax.random.fold_in(jax.random.fold_in(rng, 6), dim), (shards_of,), jnp.float32, least / len(shards), top_value / len(shards))
        return jnp.repeat(jnp.exp(heights), shape[dim] // shards_of).reshape((-1,) + (1,) * (len(shape) - dim - 1))

    gain = one(*shards[0])
    for cut in shards[1:]:
        gain = gain * one(*cut)
    return gain


def setup_inputs(seed: int = 0) -> dict:
    streams_of = jax.random.split(jax.random.key(seed), 7)
    params = draw_params(jax.random.fold_in(streams_of[6], 71), 0)
    camera = draw_camera(jax.random.fold_in(streams_of[6], 71), 0)
    targets = jnp.clip(1.0 * jax.random.uniform(streams_of[2], (CAMERA_VIEWS, NT, 3, PIX), jnp.float32) ** block_scale(streams_of[2], (CAMERA_VIEWS, NT, 3, PIX), ((0, 4), (1, 8)), -0.2, 0.2), 0.0, 1.0)
    send_blocks = draw_send_blocks(jax.random.fold_in(streams_of[6], 71), 0)
    tile_blocks = draw_tile_blocks(jax.random.fold_in(streams_of[6], 71), 0)
    tile_order = draw_tile_order(jax.random.fold_in(streams_of[6], 71), 0)
    return dict(params=params, camera=camera, targets=targets, send_blocks=send_blocks, tile_blocks=tile_blocks, tile_order=tile_order)


HIGHEST_PRECISE = lax.Precision.HIGHEST
SH_ZERO = 0.28209479177387814
SH_ONE = 0.4886025119029199
SH_TWO = [1.0925484305920792, -1.0925484305920792, 0.31539156525252005, -1.0925484305920792, 0.5462742152960396]
SH_THREE = [-0.5900435899266435, 2.890611442640554, -0.4570457994644658, 0.3731763325901154, -0.4570457994644658, 1.445305721320277, -0.5900435899266435]

def quat_matrix(qw, qx, qy, qz):
    return [[1.0 - 2.0 * (qy * qy + qz * qz), 2.0 * (qx * qy - qw * qz), 2.0 * (qx * qz + qw * qy)], [2.0 * (qx * qy + qw * qz), 1.0 - 2.0 * (qx * qx + qz * qz), 2.0 * (qy * qz - qw * qx)], [2.0 * (qx * qz - qw * qy), 2.0 * (qy * qz + qw * qx), 1.0 - 2.0 * (qx * qx + qy * qy)]]

def sh_basis(dirx, diry, dirz):
    xx, yy, zz = (dirx * dirx, diry * diry, dirz * dirz)
    return [SH_ZERO + 0.0 * dirx, -SH_ONE * diry, SH_ONE * dirz, -SH_ONE * dirx, SH_TWO[0] * dirx * diry, SH_TWO[1] * diry * dirz, SH_TWO[2] * (2.0 * zz - xx - yy), SH_TWO[3] * dirx * dirz, SH_TWO[4] * (xx - yy), SH_THREE[0] * diry * (3.0 * xx - yy), SH_THREE[1] * dirx * diry * dirz, SH_THREE[2] * diry * (4.0 * zz - xx - yy), SH_THREE[3] * dirz * (2.0 * zz - 3.0 * xx - 3.0 * yy), SH_THREE[4] * dirx * (4.0 * zz - xx - yy), SH_THREE[5] * dirz * (xx - yy), SH_THREE[6] * dirx * (xx - 3.0 * yy)]

def project(gauss, camera_row):
    cam_norm = jnp.sqrt(jnp.sum(camera_row[0:4] * camera_row[0:4]))
    cam_quat = camera_row[0:4] / cam_norm
    rotation = quat_matrix(cam_quat[0], cam_quat[1], cam_quat[2], cam_quat[3])
    focal_x, focal_y, centre_x, centre_y = (camera_row[7], camera_row[8], camera_row[9], camera_row[10])
    cam_pos = [rotation[i][0] * gauss[0] + rotation[i][1] * gauss[1] + rotation[i][2] * gauss[2] + camera_row[4 + i] for i in range(3)]
    inverse = 1.0 / cam_pos[2]
    screen_u = focal_x * cam_pos[0] * inverse + centre_x
    screen_w = focal_y * cam_pos[1] * inverse + centre_y
    gauss_norm = jnp.sqrt(gauss[6] * gauss[6] + gauss[7] * gauss[7] + gauss[8] * gauss[8] + gauss[9] * gauss[9])
    grot = quat_matrix(gauss[6] / gauss_norm, gauss[7] / gauss_norm, gauss[8] / gauss_norm, gauss[9] / gauss_norm)
    scales = [jnp.exp(gauss[3 + k]) for k in range(3)]
    axes_cam = [[rotation[i][0] * grot[0][k] + rotation[i][1] * grot[1][k] + rotation[i][2] * grot[2][k] for k in range(3)] for i in range(3)]
    row_one = [(focal_x * inverse * axes_cam[0][k] - focal_x * cam_pos[0] * inverse * inverse * axes_cam[2][k]) * scales[k] for k in range(3)]
    row_two = [(focal_y * inverse * axes_cam[1][k] - focal_y * cam_pos[1] * inverse * inverse * axes_cam[2][k]) * scales[k] for k in range(3)]
    entry_a = row_one[0] * row_one[0] + row_one[1] * row_one[1] + row_one[2] * row_one[2] + 0.3
    entry_b = row_one[0] * row_two[0] + row_one[1] * row_two[1] + row_one[2] * row_two[2]
    entry_c = row_two[0] * row_two[0] + row_two[1] * row_two[1] + row_two[2] * row_two[2] + 0.3
    determinant = entry_a * entry_c - entry_b * entry_b
    opacity = jax.nn.sigmoid(gauss[10])
    distance = jnp.sqrt(cam_pos[0] * cam_pos[0] + cam_pos[1] * cam_pos[1] + cam_pos[2] * cam_pos[2])
    direction = [(rotation[0][j] * cam_pos[0] + rotation[1][j] * cam_pos[1] + rotation[2][j] * cam_pos[2]) / distance for j in range(3)]
    basis = sh_basis(direction[0], direction[1], direction[2])
    colors = []
    for channel in range(3):
        accum = 0.5 + basis[0] * gauss[11 + channel]
        for order in range(1, 16):
            accum = accum + basis[order] * gauss[11 + 3 * order + channel]
        colors.append(jnp.maximum(accum, 0.0))
    return jnp.stack([screen_u, screen_w, entry_c / determinant, -entry_b / determinant, entry_a / determinant, opacity] + colors)

def expand(blocks, order):
    tiles_n, width = blocks.shape
    visible = blocks >= 0
    slots = jnp.maximum(blocks, 0).astype(jnp.int32)
    inner_product = jnp.arange(BLOCK_GAUSSIANS, dtype=jnp.int32)
    positions = (slots[:, :, None] * BLOCK_GAUSSIANS + inner_product).reshape(tiles_n, width * BLOCK_GAUSSIANS)
    visible = jnp.broadcast_to(visible[:, :, None], (tiles_n, width, BLOCK_GAUSSIANS)).reshape(tiles_n, width * BLOCK_GAUSSIANS)
    positions = jnp.take_along_axis(positions, order.astype(jnp.int32), axis=1)
    visible = jnp.take_along_axis(visible, order.astype(jnp.int32), axis=1)
    return (positions, visible)

def composite(fields, positions, visible, goal, first_tile):
    count, length = positions.shape
    pixels = goal.shape[-1]
    group = math.gcd(count, 8)
    steps_n = count // group
    pixel_ids = jnp.arange(pixels, dtype=jnp.int32)
    offset_x = (pixel_ids % 16).astype(jnp.float32) + 0.5
    offset_y = (pixel_ids // 16).astype(jnp.float32) + 0.5

    def step(carry, item):
        indices, alive, wanted, number = item
        tiles = first_tile + number * group + jnp.arange(group, dtype=jnp.int32)
        pix_x = (tiles % TX * 16).astype(jnp.float32)[:, None] + offset_x
        pix_y = (tiles // TX * 16).astype(jnp.float32)[:, None] + offset_y
        weights_mask = alive.astype(jnp.float32)

        def render(local_part):
            delta_x = pix_x[:, None, :] - local_part[0][:, :, None]
            delta_y = pix_y[:, None, :] - local_part[1][:, :, None]
            power = -0.5 * (local_part[2][:, :, None] * delta_x * delta_x + local_part[4][:, :, None] * delta_y * delta_y) - local_part[3][:, :, None] * delta_x * delta_y
            alpha_value = (local_part[5] * weights_mask)[:, :, None] * jnp.exp(power)
            logs = jnp.log1p(-alpha_value)
            transmit_factor = jnp.exp(jnp.cumsum(logs, axis=1) - logs)
            return jnp.einsum('dal,jda->djl', alpha_value * transmit_factor, local_part[6:9], precision=HIGHEST_PRECISE)
        local_part = fields[:, indices]
        color, pullback = jax.vjp(render, local_part)
        local_grad = pullback((color - wanted) / pixels)[0]
        carry = carry.at[:, indices.reshape(-1)].add(local_grad.reshape(local_grad.shape[0], -1))
        return (carry, color)
    items = (positions.reshape(steps_n, group, length), visible.reshape(steps_n, group, length), goal.reshape(steps_n, group, 3, pixels), jnp.arange(steps_n, dtype=jnp.int32))
    total, colors = lax.scan(step, jnp.zeros_like(fields), items)
    return (colors.reshape(count, 3, pixels), total)

def reference(params, camera, targets, send_blocks, tile_blocks, tile_order):
    grads = jnp.zeros(params.shape, jnp.float32)
    images = []
    inner_product = jnp.arange(BLOCK_GAUSSIANS, dtype=jnp.int32)
    owners = jnp.arange(NT, dtype=jnp.int32) // TILES_PER_DEVICE
    for view_id in range(CAMERA_VIEWS):
        camera_row = camera[view_id]
        fields, pullback = jax.vjp(lambda gathered: project(gathered, camera_row), params)
        base_offset = (jnp.arange(N_CELL, dtype=jnp.int32) * G_DEV)[:, None, None] + send_blocks[view_id].astype(jnp.int32) * BLOCK_GAUSSIANS
        lookup_table = (jnp.transpose(base_offset, (1, 0, 2))[..., None] + inner_product).reshape(N_CELL, RECEIVED_SLOTS * BLOCK_GAUSSIANS)
        positions, visible = expand(tile_blocks[view_id], tile_order[view_id])
        gauss_ids = lookup_table[owners[:, None], positions]
        picture, field_grad = composite(fields, gauss_ids, visible, targets[view_id], 0)
        grads = grads + pullback(field_grad)[0]
        images.append(picture)
    return (jnp.stack(images), grads)
```

```python
import jax
import numpy as np
import jax.numpy as jnp
from jax import lax
from jax.experimental import pallas as pl
from jax.experimental.pallas import tpu as pltpu
from jax.sharding import PartitionSpec as P

BLOCK_GAUSSIANS = 32
TX = 32


HIGHEST_PRECISE = lax.Precision.HIGHEST
SH_ZERO = 0.28209479177387814
SH_ONE = 0.4886025119029199
SH_TWO = [
    1.0925484305920792,
    -1.0925484305920792,
    0.31539156525252005,
    -1.0925484305920792,
    0.5462742152960396,
]
SH_THREE = [
    -0.5900435899266435,
    2.890611442640554,
    -0.4570457994644658,
    0.3731763325901154,
    -0.4570457994644658,
    1.445305721320277,
    -0.5900435899266435,
]


def quat_matrix(qw, qx, qy, qz):
    return [
        [1.0 - 2.0 * (qy * qy + qz * qz), 2.0 * (qx * qy - qw * qz), 2.0 * (qx * qz + qw * qy)],
        [2.0 * (qx * qy + qw * qz), 1.0 - 2.0 * (qx * qx + qz * qz), 2.0 * (qy * qz - qw * qx)],
        [2.0 * (qx * qz - qw * qy), 2.0 * (qy * qz + qw * qx), 1.0 - 2.0 * (qx * qx + qy * qy)],
    ]


def sh_basis(dirx, diry, dirz):
    xx, yy, zz = (dirx * dirx, diry * diry, dirz * dirz)
    return [
        SH_ZERO + 0.0 * dirx,
        -SH_ONE * diry,
        SH_ONE * dirz,
        -SH_ONE * dirx,
        SH_TWO[0] * dirx * diry,
        SH_TWO[1] * diry * dirz,
        SH_TWO[2] * (2.0 * zz - xx - yy),
        SH_TWO[3] * dirx * dirz,
        SH_TWO[4] * (xx - yy),
        SH_THREE[0] * diry * (3.0 * xx - yy),
        SH_THREE[1] * dirx * diry * dirz,
        SH_THREE[2] * diry * (4.0 * zz - xx - yy),
        SH_THREE[3] * dirz * (2.0 * zz - 3.0 * xx - 3.0 * yy),
        SH_THREE[4] * dirx * (4.0 * zz - xx - yy),
        SH_THREE[5] * dirz * (xx - yy),
        SH_THREE[6] * dirx * (xx - 3.0 * yy),
    ]


def project(gauss, camera_row):
    cam_norm = jnp.sqrt(jnp.sum(camera_row[0:4] * camera_row[0:4]))
    cam_quat = camera_row[0:4] / cam_norm
    rotation = quat_matrix(cam_quat[0], cam_quat[1], cam_quat[2], cam_quat[3])
    focal_x, focal_y, centre_x, centre_y = (
        camera_row[7],
        camera_row[8],
        camera_row[9],
        camera_row[10],
    )
    cam_pos = [
        rotation[i][0] * gauss[0]
        + rotation[i][1] * gauss[1]
        + rotation[i][2] * gauss[2]
        + camera_row[4 + i]
        for i in range(3)
    ]
    inverse = 1.0 / cam_pos[2]
    screen_u = focal_x * cam_pos[0] * inverse + centre_x
    screen_w = focal_y * cam_pos[1] * inverse + centre_y
    gauss_norm = jnp.sqrt(
        gauss[6] * gauss[6] + gauss[7] * gauss[7] + gauss[8] * gauss[8] + gauss[9] * gauss[9]
    )
    grot = quat_matrix(
        gauss[6] / gauss_norm, gauss[7] / gauss_norm, gauss[8] / gauss_norm, gauss[9] / gauss_norm
    )
    scales = [jnp.exp(gauss[3 + k]) for k in range(3)]
    axes_cam = [
        [
            rotation[i][0] * grot[0][k] + rotation[i][1] * grot[1][k] + rotation[i][2] * grot[2][k]
            for k in range(3)
        ]
        for i in range(3)
    ]
    row_one = [
        (
            focal_x * inverse * axes_cam[0][k]
            - focal_x * cam_pos[0] * inverse * inverse * axes_cam[2][k]
        )
        * scales[k]
        for k in range(3)
    ]
    row_two = [
        (
            focal_y * inverse * axes_cam[1][k]
            - focal_y * cam_pos[1] * inverse * inverse * axes_cam[2][k]
        )
        * scales[k]
        for k in range(3)
    ]
    entry_a = row_one[0] * row_one[0] + row_one[1] * row_one[1] + row_one[2] * row_one[2] + 0.3
    entry_b = row_one[0] * row_two[0] + row_one[1] * row_two[1] + row_one[2] * row_two[2]
    entry_c = row_two[0] * row_two[0] + row_two[1] * row_two[1] + row_two[2] * row_two[2] + 0.3
    determinant = entry_a * entry_c - entry_b * entry_b
    opacity = jax.nn.log_sigmoid(gauss[10])
    distance = jnp.sqrt(cam_pos[0] * cam_pos[0] + cam_pos[1] * cam_pos[1] + cam_pos[2] * cam_pos[2])
    direction = [
        (rotation[0][j] * cam_pos[0] + rotation[1][j] * cam_pos[1] + rotation[2][j] * cam_pos[2])
        / distance
        for j in range(3)
    ]
    basis = sh_basis(direction[0], direction[1], direction[2])
    colors = []
    for channel in range(3):
        accum = 0.5 + basis[0] * gauss[11 + channel]
        for order in range(1, 16):
            accum = accum + basis[order] * gauss[11 + 3 * order + channel]
        colors.append(jnp.maximum(accum, 0.0))
    return jnp.stack(
        [
            screen_u,
            screen_w,
            entry_c / determinant,
            -entry_b / determinant,
            entry_a / determinant,
            opacity,
        ]
        + colors
    )


TILE = 16
GROUP = 8
ROWS = 16
FIELDS = 9
NT_DIMS = (((1,), (1,)), ((), ()))


def pieces3(values):
    one = values.astype(jnp.bfloat16).astype(jnp.float32)
    rest = values - one
    two = rest.astype(jnp.bfloat16).astype(jnp.float32)
    return one, two, rest - two


def basis_rows(pixels):
    ids = np.arange(pixels)
    px = ids % TILE + 0.5 - TILE / 2
    py = ids // TILE + 0.5 - TILE / 2
    return np.stack([np.ones(pixels), px, py, px * px, px * py, py * py]).astype(np.float32)


def composite_kernel(
    slots_ref, first_ref, tab_ref, ord_ref, tgt_ref, wmat_ref, bas_ref, img_ref, gt_ref,
    p_s, f_s, x_s, m_s, w_s, y_s,
):
    group = pl.program_id(0)
    length = ord_ref.shape[1]
    pixels = tgt_ref.shape[2]
    entries = slots_ref.shape[1]
    per = 128 // BLOCK_GAUSSIANS

    @pl.when(group == 0)
    def _():
        gt_ref[...] = jnp.zeros_like(gt_ref)

    lane_part = lax.broadcasted_iota(jnp.int32, (ROWS, 128), 1) // BLOCK_GAUSSIANS
    lane_ids = lax.broadcasted_iota(jnp.int32, (length, length), 1)
    tile0 = first_ref[0] + group * GROUP

    def centre(t):
        tile = tile0 + t
        cx = (lax.rem(tile, TX) * TILE + TILE // 2).astype(jnp.float32)
        cy = (lax.div(tile, TX) * TILE + TILE // 2).astype(jnp.float32)
        return cx, cy

    for t in range(GROUP):
        cols = []
        for v in range(entries // per):
            chunk = None
            for b in range(per):
                block = tab_ref[slots_ref[group * GROUP + t, v * per + b]]
                chunk = block if chunk is None else jnp.where(lane_part == b, block, chunk)
            cols.append(chunk)
        fields = jnp.concatenate(cols, axis=1)
        cx, cy = centre(t)
        u = fields[0:1] - cx
        w = fields[1:2] - cy
        con_a, con_b, con_c, logo = fields[2:3], fields[3:4], fields[4:5], fields[5:6]
        f_s[t] = fields
        coefs = jnp.concatenate(
            [
                logo - 0.5 * (con_a * u * u + con_c * w * w) - con_b * u * w,
                con_a * u + con_b * w,
                con_c * w + con_b * u,
                -0.5 * con_a,
                -con_b,
                -0.5 * con_c,
                fields[6:9],
                jnp.zeros((ROWS - FIELDS, length), jnp.float32),
            ],
            axis=0,
        )
        parts = jnp.concatenate(
            list(pieces3(coefs)) + [jnp.zeros((128 - 3 * ROWS, length), jnp.float32)], axis=0
        ).astype(jnp.bfloat16)
        perm = jnp.where(ord_ref[0, :, t : t + 1] == lane_ids, 1.0, 0.0).astype(jnp.bfloat16)
        p_s[t] = perm
        x_s[pl.ds(t, length, stride=GROUP), :] = lax.dot_general(
            perm, parts, NT_DIMS, preferred_element_type=jnp.float32
        )

    rows = 64 * GROUP
    steps = length * GROUP // rows

    @pl.loop(0, steps)
    def _(c):
        part = pl.ds(pl.multiple_of(c * rows, rows), rows)
        m_s[part, :] = jnp.dot(
            x_s[part, :].astype(jnp.bfloat16), wmat_ref[...], preferred_element_type=jnp.float32
        )

    def twice(x):
        return jnp.concatenate([x] * (pixels // 128), axis=1)

    def load_colors(r):
        return [twice(m_s[r, pixels + 128 * ch : pixels + 128 * (ch + 1)]) for ch in range(3)]

    def forward(k, carry):
        trans, acc = carry
        r = pl.ds(pl.multiple_of(k * GROUP, GROUP), GROUP)
        alpha = jnp.exp(m_s[r, 0:pixels])
        weight = alpha * trans
        m_s[r, 0:pixels] = alpha
        w_s[r, :] = weight
        colors = load_colors(r)
        acc = tuple(a + c * weight for a, c in zip(acc, colors))
        return (trans - weight, acc)

    zero = jnp.zeros((GROUP, pixels), jnp.float32)
    _, image = lax.fori_loop(0, length, forward, (zero + 1.0, (zero, zero, zero)), unroll=8)
    glist = []
    for ch in range(3):
        img_ref[ch] = image[ch]
        glist.append((image[ch] - tgt_ref[ch]) * (1.0 / pixels))

    def backward(i, carry):
        k = length - 1 - i
        r = pl.ds(pl.multiple_of(k * GROUP, GROUP), GROUP)
        alpha = m_s[r, 0:pixels]
        weight = w_s[r, :]
        c = load_colors(r)
        dot = c[0] * glist[0] + c[1] * glist[1] + c[2] * glist[2]
        term = weight * dot
        m_s[r, 0:pixels] = term - carry * (alpha / (1.0 - alpha))
        return carry + term

    lax.fori_loop(0, length, backward, zero, unroll=8)

    grows = jnp.concatenate(
        [jnp.zeros((16, pixels), jnp.float32)]
        + glist
        + [jnp.zeros((128 - 16 - 3 * GROUP, pixels), jnp.float32)],
        axis=0,
    )
    ghigh = grows.astype(jnp.bfloat16)
    glow = (grows - ghigh.astype(jnp.float32)).astype(jnp.bfloat16)

    def nt(a, b):
        return lax.dot_general(a, b, NT_DIMS, preferred_element_type=jnp.float32)

    @pl.loop(0, steps)
    def _(c):
        part = pl.ds(pl.multiple_of(c * rows, rows), rows)
        h = m_s[part, 0:pixels]
        weight = w_s[part, :]
        h1 = h.astype(jnp.bfloat16)
        h2 = (h - h1.astype(jnp.float32)).astype(jnp.bfloat16)
        w1 = weight.astype(jnp.bfloat16)
        w2 = (weight - w1.astype(jnp.float32)).astype(jnp.bfloat16)
        bas = bas_ref[...]
        y_s[part, :] = nt(h1, bas) + nt(h2, bas) + nt(w1, ghigh) + nt(w1, glow) + nt(w2, ghigh)

    used = 16 + 3 * GROUP
    for t in range(GROUP):
        moments = y_s[pl.ds(t, length, stride=GROUP), :].T[0:used]
        stacked = jnp.concatenate(
            list(pieces3(moments)) + [jnp.zeros((128 - 3 * used, length), jnp.float32)], axis=0
        ).astype(jnp.bfloat16)
        back = jnp.dot(stacked, p_s[t], preferred_element_type=jnp.float32)
        back = back[0:used] + back[used : 2 * used] + back[2 * used : 3 * used]
        fields = f_s[t]
        cx, cy = centre(t)
        u = fields[0:1] - cx
        w = fields[1:2] - cy
        con_a, con_b, con_c = fields[2:3], fields[3:4], fields[4:5]
        h0, hx, hy, hxx, hxy, hyy = [back[j : j + 1] for j in range(6)]
        sx = hx - u * h0
        sy = hy - w * h0
        sxx = hxx - 2.0 * u * hx + u * u * h0
        syy = hyy - 2.0 * w * hy + w * w * h0
        sxy = hxy - u * hy - w * hx + u * w * h0
        out = jnp.concatenate(
            [
                con_a * sx + con_b * sy,
                con_c * sy + con_b * sx,
                -0.5 * sxx,
                -sxy,
                -0.5 * syy,
                h0,
            ]
            + [back[16 + ch * GROUP + t : 17 + ch * GROUP + t] for ch in range(3)]
            + [jnp.zeros((ROWS - FIELDS, length), jnp.float32)],
            axis=0,
        )
        for e in range(entries):
            slot = slots_ref[group * GROUP + t, e]
            v, b = divmod(e, per)
            gt_ref[slot] += jnp.where(lane_part == b, out[:, v * 128 : (v + 1) * 128], 0.0)


def composite(table, slots, order, goal, first_tile):
    tiles, length = order.shape
    pixels = goal.shape[-1]
    groups = tiles // GROUP
    table_rows = table.shape[0]
    order_cols = jnp.transpose(order.reshape(groups, GROUP, length), (0, 2, 1))
    basis = basis_rows(pixels)
    wmat = np.zeros((128, pixels + 3 * 128), np.float32)
    for piece in range(3):
        wmat[piece * ROWS : piece * ROWS + 6, :pixels] = basis
        for ch in range(3):
            wmat[piece * ROWS + 6 + ch, pixels + 128 * ch : pixels + 128 * (ch + 1)] = 1.0
    bas = np.zeros((128, pixels), np.float32)
    bas[:6] = basis
    full = lambda g, *_: (0, 0)
    whole = lambda g, *_: (0, 0, 0)
    image, gtab = pl.pallas_call(
        composite_kernel,
        out_shape=(
            jax.ShapeDtypeStruct((3, tiles, pixels), jnp.float32),
            jax.ShapeDtypeStruct((table_rows, ROWS, 128), jnp.float32),
        ),
        grid_spec=pltpu.PrefetchScalarGridSpec(
            num_scalar_prefetch=2,
            grid=(groups,),
            in_specs=[
                pl.BlockSpec((table_rows, ROWS, 128), whole),
                pl.BlockSpec((1, length, GROUP), lambda g, *_: (g, 0, 0)),
                pl.BlockSpec((3, GROUP, pixels), lambda g, *_: (0, g, 0)),
                pl.BlockSpec(wmat.shape, full),
                pl.BlockSpec(bas.shape, full),
            ],
            out_specs=(
                pl.BlockSpec((3, GROUP, pixels), lambda g, *_: (0, g, 0)),
                pl.BlockSpec((table_rows, ROWS, 128), whole),
            ),
            scratch_shapes=[
                pltpu.VMEM((GROUP, length, length), jnp.bfloat16),
                pltpu.VMEM((GROUP, ROWS, length), jnp.float32),
                pltpu.VMEM((length * GROUP, 128), jnp.float32),
                pltpu.VMEM((length * GROUP, pixels + 3 * 128), jnp.float32),
                pltpu.VMEM((length * GROUP, pixels), jnp.float32),
                pltpu.VMEM((length * GROUP, 128), jnp.float32),
            ],
        ),
        compiler_params=pltpu.CompilerParams(
            dimension_semantics=("arbitrary",), vmem_limit_bytes=60 * 1024 * 1024
        ),
    )(
        slots,
        first_tile,
        table,
        order_cols,
        jnp.transpose(goal, (1, 0, 2)),
        jnp.asarray(wmat, jnp.bfloat16),
        jnp.asarray(bas, jnp.bfloat16),
    )
    return jnp.transpose(image, (1, 0, 2)), gtab


def local(params, camera, targets, send_blocks, tile_blocks, tile_order):
    cells = lax.axis_size("cell")
    views = lax.axis_size("view")
    cell_index = lax.axis_index("cell")
    owned = params.shape[1]
    owned_blocks = owned // BLOCK_GAUSSIANS
    per_peer = send_blocks.shape[3]
    slots_n = cells * per_peer
    block_values = FIELDS * BLOCK_GAUSSIANS
    picks = send_blocks[0, 0].reshape(-1)
    cameras = lax.all_gather(camera[0], "view")
    fields = project(params, camera[0])
    by_block = jnp.transpose(
        fields.reshape(FIELDS, owned_blocks, BLOCK_GAUSSIANS), (1, 0, 2)
    ).reshape(owned_blocks, block_values)
    chosen = jnp.take(by_block, picks, axis=0).reshape(cells, per_peer * block_values)
    received = lax.all_to_all(chosen, "cell", split_axis=0, concat_axis=0, tiled=True)
    received = received.reshape(slots_n, FIELDS, BLOCK_GAUSSIANS)
    dummy = np.zeros((1, FIELDS, BLOCK_GAUSSIANS), np.float32)
    dummy[:, 5] = -1e30
    table = jnp.concatenate([received, jnp.asarray(dummy)], axis=0)
    table = jnp.tile(
        jnp.pad(table, ((0, 0), (0, ROWS - FIELDS), (0, 0))), (1, 1, 128 // BLOCK_GAUSSIANS)
    )
    blocks = tile_blocks[0]
    slots = jnp.where(blocks < 0, slots_n, blocks)
    first_tile = (cell_index * blocks.shape[0]).astype(jnp.int32).reshape(1)
    picture, gtab = composite(table, slots, tile_order[0], targets[0], first_tile)
    slot_grad = (
        gtab[:slots_n, :FIELDS]
        .reshape(slots_n, FIELDS, 128 // BLOCK_GAUSSIANS, BLOCK_GAUSSIANS)
        .sum(2)
        .reshape(cells, per_peer * block_values)
    )
    returned = lax.all_to_all(slot_grad, "cell", split_axis=0, concat_axis=0, tiled=True)
    chosen_of = (jnp.arange(owned_blocks)[:, None] == picks[None, :]).astype(jnp.float32)
    summed = jnp.dot(
        chosen_of, returned.reshape(slots_n, block_values), precision=HIGHEST_PRECISE
    )
    quarter = owned // views
    summed = jnp.transpose(
        summed.reshape(owned_blocks, FIELDS, BLOCK_GAUSSIANS), (1, 0, 2)
    ).reshape(FIELDS, views, quarter)
    by_view = lax.all_to_all(summed, "view", split_axis=1, concat_axis=1, tiled=True)
    mine = lax.dynamic_slice_in_dim(params, lax.axis_index("view") * quarter, quarter, axis=1)
    _, pullback = jax.vjp(
        lambda p: [project(p, cameras[v]) for v in range(views)], mine
    )
    part = pullback([by_view[:, v] for v in range(views)])[0]
    total = lax.all_gather(part, "view", axis=1, tiled=True)
    return (picture[None], total)


def solution(mesh):
    return jax.shard_map(
        local,
        mesh=mesh,
        in_specs=(
            P(None, "cell"),
            P("view", None),
            P("view", "cell", None, None),
            P("view", "cell", None, None),
            P("view", "cell", None),
            P("view", "cell", None),
        ),
        out_specs=(P("view", "cell", None, None), P(None, "cell")),
        check_vma=False,
    )
```

```python
import jax
import numpy as np
import jax.numpy as jnp
from jax import lax
from jax.experimental import pallas as pl
from jax.experimental.pallas import tpu as pltpu
from jax.sharding import PartitionSpec as P

BLOCK_GAUSSIANS = 32
TX = 32


HIGHEST_PRECISE = lax.Precision.HIGHEST
SH_ZERO = 0.28209479177387814
SH_ONE = 0.4886025119029199
SH_TWO = [
    1.0925484305920792,
    -1.0925484305920792,
    0.31539156525252005,
    -1.0925484305920792,
    0.5462742152960396,
]
SH_THREE = [
    -0.5900435899266435,
    2.890611442640554,
    -0.4570457994644658,
    0.3731763325901154,
    -0.4570457994644658,
    1.445305721320277,
    -0.5900435899266435,
]


def quat_matrix(qw, qx, qy, qz):
    return [
        [1.0 - 2.0 * (qy * qy + qz * qz), 2.0 * (qx * qy - qw * qz), 2.0 * (qx * qz + qw * qy)],
        [2.0 * (qx * qy + qw * qz), 1.0 - 2.0 * (qx * qx + qz * qz), 2.0 * (qy * qz - qw * qx)],
        [2.0 * (qx * qz - qw * qy), 2.0 * (qy * qz + qw * qx), 1.0 - 2.0 * (qx * qx + qy * qy)],
    ]


def sh_basis(dirx, diry, dirz):
    xx, yy, zz = (dirx * dirx, diry * diry, dirz * dirz)
    return [
        SH_ZERO + 0.0 * dirx,
        -SH_ONE * diry,
        SH_ONE * dirz,
        -SH_ONE * dirx,
        SH_TWO[0] * dirx * diry,
        SH_TWO[1] * diry * dirz,
        SH_TWO[2] * (2.0 * zz - xx - yy),
        SH_TWO[3] * dirx * dirz,
        SH_TWO[4] * (xx - yy),
        SH_THREE[0] * diry * (3.0 * xx - yy),
        SH_THREE[1] * dirx * diry * dirz,
        SH_THREE[2] * diry * (4.0 * zz - xx - yy),
        SH_THREE[3] * dirz * (2.0 * zz - 3.0 * xx - 3.0 * yy),
        SH_THREE[4] * dirx * (4.0 * zz - xx - yy),
        SH_THREE[5] * dirz * (xx - yy),
        SH_THREE[6] * dirx * (xx - 3.0 * yy),
    ]


def project(gauss, camera_row):
    cam_norm = jnp.sqrt(
        camera_row[0] * camera_row[0]
        + camera_row[1] * camera_row[1]
        + camera_row[2] * camera_row[2]
        + camera_row[3] * camera_row[3]
    )
    cam_quat = [camera_row[i] / cam_norm for i in range(4)]
    rotation = quat_matrix(cam_quat[0], cam_quat[1], cam_quat[2], cam_quat[3])
    focal_x, focal_y, centre_x, centre_y = (
        camera_row[7],
        camera_row[8],
        camera_row[9],
        camera_row[10],
    )
    cam_pos = [
        rotation[i][0] * gauss[0]
        + rotation[i][1] * gauss[1]
        + rotation[i][2] * gauss[2]
        + camera_row[4 + i]
        for i in range(3)
    ]
    inverse = 1.0 / cam_pos[2]
    screen_u = focal_x * cam_pos[0] * inverse + centre_x
    screen_w = focal_y * cam_pos[1] * inverse + centre_y
    gauss_norm = jnp.sqrt(
        gauss[6] * gauss[6] + gauss[7] * gauss[7] + gauss[8] * gauss[8] + gauss[9] * gauss[9]
    )
    grot = quat_matrix(
        gauss[6] / gauss_norm, gauss[7] / gauss_norm, gauss[8] / gauss_norm, gauss[9] / gauss_norm
    )
    scales = [jnp.exp(gauss[3 + k]) for k in range(3)]
    axes_cam = [
        [
            rotation[i][0] * grot[0][k] + rotation[i][1] * grot[1][k] + rotation[i][2] * grot[2][k]
            for k in range(3)
        ]
        for i in range(3)
    ]
    row_one = [
        (
            focal_x * inverse * axes_cam[0][k]
            - focal_x * cam_pos[0] * inverse * inverse * axes_cam[2][k]
        )
        * scales[k]
        for k in range(3)
    ]
    row_two = [
        (
            focal_y * inverse * axes_cam[1][k]
            - focal_y * cam_pos[1] * inverse * inverse * axes_cam[2][k]
        )
        * scales[k]
        for k in range(3)
    ]
    entry_a = row_one[0] * row_one[0] + row_one[1] * row_one[1] + row_one[2] * row_one[2] + 0.3
    entry_b = row_one[0] * row_two[0] + row_one[1] * row_two[1] + row_one[2] * row_two[2]
    entry_c = row_two[0] * row_two[0] + row_two[1] * row_two[1] + row_two[2] * row_two[2] + 0.3
    determinant = entry_a * entry_c - entry_b * entry_b
    opacity = -jnp.log(1.0 + jnp.exp(-gauss[10]))
    distance = jnp.sqrt(cam_pos[0] * cam_pos[0] + cam_pos[1] * cam_pos[1] + cam_pos[2] * cam_pos[2])
    direction = [
        (rotation[0][j] * cam_pos[0] + rotation[1][j] * cam_pos[1] + rotation[2][j] * cam_pos[2])
        / distance
        for j in range(3)
    ]
    basis = sh_basis(direction[0], direction[1], direction[2])
    colors = []
    for channel in range(3):
        accum = 0.5 + basis[0] * gauss[11 + channel]
        for order in range(1, 16):
            accum = accum + basis[order] * gauss[11 + 3 * order + channel]
        colors.append(jnp.maximum(accum, 0.0))
    return [
        screen_u,
        screen_w,
        entry_c / determinant,
        -entry_b / determinant,
        entry_a / determinant,
        opacity,
    ] + colors


TILE = 16
GROUP = 8
ROWS = 16
FIELDS = 9
NT_DIMS = (((1,), (1,)), ((), ()))


def pieces3(values):
    one = values.astype(jnp.bfloat16).astype(jnp.float32)
    rest = values - one
    two = rest.astype(jnp.bfloat16).astype(jnp.float32)
    return one, two, rest - two


def basis_rows(pixels):
    ids = np.arange(pixels)
    px = ids % TILE + 0.5 - TILE / 2
    py = ids // TILE + 0.5 - TILE / 2
    return np.stack([np.ones(pixels), px, py, px * px, px * py, py * py]).astype(np.float32)


def composite_kernel(
    slots_ref, first_ref, tab_ref, ord_ref, tgt_ref, wmat_ref, bas_ref, img_ref, gt_ref,
    p_s, f_s, x_s, m_s, w_s, y_s,
):
    group = pl.program_id(0)
    length = ord_ref.shape[1]
    pixels = tgt_ref.shape[2]
    entries = slots_ref.shape[1]
    per = 128 // BLOCK_GAUSSIANS

    @pl.when(group == 0)
    def _():
        gt_ref[...] = jnp.zeros_like(gt_ref)

    lane_part = lax.broadcasted_iota(jnp.int32, (ROWS, 128), 1) // BLOCK_GAUSSIANS
    lane_ids = lax.broadcasted_iota(jnp.int32, (length, length), 1)
    tile0 = first_ref[0] + group * GROUP

    def centre(t):
        tile = tile0 + t
        cx = (lax.rem(tile, TX) * TILE + TILE // 2).astype(jnp.float32)
        cy = (lax.div(tile, TX) * TILE + TILE // 2).astype(jnp.float32)
        return cx, cy

    for t in range(GROUP):
        cols = []
        for v in range(entries // per):
            chunk = None
            for b in range(per):
                block = tab_ref[slots_ref[group * GROUP + t, v * per + b]]
                chunk = block if chunk is None else jnp.where(lane_part == b, block, chunk)
            cols.append(chunk)
        fields = jnp.concatenate(cols, axis=1)
        cx, cy = centre(t)
        u = fields[0:1] - cx
        w = fields[1:2] - cy
        con_a, con_b, con_c, logo = fields[2:3], fields[3:4], fields[4:5], fields[5:6]
        f_s[t] = fields
        coefs = jnp.concatenate(
            [
                logo - 0.5 * (con_a * u * u + con_c * w * w) - con_b * u * w,
                con_a * u + con_b * w,
                con_c * w + con_b * u,
                -0.5 * con_a,
                -con_b,
                -0.5 * con_c,
                fields[6:9],
                jnp.zeros((ROWS - FIELDS, length), jnp.float32),
            ],
            axis=0,
        )
        parts = jnp.concatenate(
            list(pieces3(coefs)) + [jnp.zeros((128 - 3 * ROWS, length), jnp.float32)], axis=0
        ).astype(jnp.bfloat16)
        perm = jnp.where(ord_ref[0, :, t : t + 1] == lane_ids, 1.0, 0.0).astype(jnp.bfloat16)
        p_s[t] = perm
        x_s[pl.ds(t, length, stride=GROUP), :] = lax.dot_general(
            perm, parts, NT_DIMS, preferred_element_type=jnp.float32
        )

    rows = 64 * GROUP
    steps = length * GROUP // rows

    @pl.loop(0, steps)
    def _(c):
        part = pl.ds(pl.multiple_of(c * rows, rows), rows)
        m_s[part, :] = jnp.dot(
            x_s[part, :].astype(jnp.bfloat16), wmat_ref[...], preferred_element_type=jnp.float32
        )

    def twice(x):
        return jnp.concatenate([x] * (pixels // 128), axis=1)

    def load_colors(r):
        return [twice(m_s[r, pixels + 128 * ch : pixels + 128 * (ch + 1)]) for ch in range(3)]

    def forward(k, carry):
        trans, acc = carry
        r = pl.ds(pl.multiple_of(k * GROUP, GROUP), GROUP)
        alpha = jnp.exp(m_s[r, 0:pixels])
        weight = alpha * trans
        m_s[r, 0:pixels] = alpha
        w_s[r, :] = weight
        colors = load_colors(r)
        acc = tuple(a + c * weight for a, c in zip(acc, colors))
        return (trans - weight, acc)

    zero = jnp.zeros((GROUP, pixels), jnp.float32)
    _, image = lax.fori_loop(0, length, forward, (zero + 1.0, (zero, zero, zero)), unroll=8)
    glist = []
    for ch in range(3):
        img_ref[ch] = image[ch]
        glist.append((image[ch] - tgt_ref[ch]) * (1.0 / pixels))

    def backward(i, carry):
        k = length - 1 - i
        r = pl.ds(pl.multiple_of(k * GROUP, GROUP), GROUP)
        alpha = m_s[r, 0:pixels]
        weight = w_s[r, :]
        c = load_colors(r)
        dot = c[0] * glist[0] + c[1] * glist[1] + c[2] * glist[2]
        term = weight * dot
        m_s[r, 0:pixels] = term - carry * (alpha / (1.0 - alpha))
        return carry + term

    lax.fori_loop(0, length, backward, zero, unroll=8)

    grows = jnp.concatenate(
        [jnp.zeros((16, pixels), jnp.float32)]
        + glist
        + [jnp.zeros((128 - 16 - 3 * GROUP, pixels), jnp.float32)],
        axis=0,
    )
    ghigh = grows.astype(jnp.bfloat16)
    glow = (grows - ghigh.astype(jnp.float32)).astype(jnp.bfloat16)

    def nt(a, b):
        return lax.dot_general(a, b, NT_DIMS, preferred_element_type=jnp.float32)

    @pl.loop(0, steps)
    def _(c):
        part = pl.ds(pl.multiple_of(c * rows, rows), rows)
        h = m_s[part, 0:pixels]
        weight = w_s[part, :]
        h1 = h.astype(jnp.bfloat16)
        h2 = (h - h1.astype(jnp.float32)).astype(jnp.bfloat16)
        w1 = weight.astype(jnp.bfloat16)
        w2 = (weight - w1.astype(jnp.float32)).astype(jnp.bfloat16)
        bas = bas_ref[...]
        y_s[part, :] = nt(h1, bas) + nt(h2, bas) + nt(w1, ghigh) + nt(w1, glow) + nt(w2, ghigh)

    used = 16 + 3 * GROUP
    for t in range(GROUP):
        moments = y_s[pl.ds(t, length, stride=GROUP), :].T[0:used]
        stacked = jnp.concatenate(
            list(pieces3(moments)) + [jnp.zeros((128 - 3 * used, length), jnp.float32)], axis=0
        ).astype(jnp.bfloat16)
        back = jnp.dot(stacked, p_s[t], preferred_element_type=jnp.float32)
        back = back[0:used] + back[used : 2 * used] + back[2 * used : 3 * used]
        fields = f_s[t]
        cx, cy = centre(t)
        u = fields[0:1] - cx
        w = fields[1:2] - cy
        con_a, con_b, con_c = fields[2:3], fields[3:4], fields[4:5]
        h0, hx, hy, hxx, hxy, hyy = [back[j : j + 1] for j in range(6)]
        sx = hx - u * h0
        sy = hy - w * h0
        sxx = hxx - 2.0 * u * hx + u * u * h0
        syy = hyy - 2.0 * w * hy + w * w * h0
        sxy = hxy - u * hy - w * hx + u * w * h0
        out = jnp.concatenate(
            [
                con_a * sx + con_b * sy,
                con_c * sy + con_b * sx,
                -0.5 * sxx,
                -sxy,
                -0.5 * syy,
                h0,
            ]
            + [back[16 + ch * GROUP + t : 17 + ch * GROUP + t] for ch in range(3)]
            + [jnp.zeros((ROWS - FIELDS, length), jnp.float32)],
            axis=0,
        )
        for e in range(entries):
            slot = slots_ref[group * GROUP + t, e]
            v, b = divmod(e, per)
            gt_ref[slot] += jnp.where(lane_part == b, out[:, v * 128 : (v + 1) * 128], 0.0)


def composite(table, slots, order, goal, first_tile):
    tiles, length = order.shape
    pixels = goal.shape[-1]
    groups = tiles // GROUP
    table_rows = table.shape[0]
    order_cols = jnp.transpose(order.reshape(groups, GROUP, length), (0, 2, 1))
    basis = basis_rows(pixels)
    wmat = np.zeros((128, pixels + 3 * 128), np.float32)
    for piece in range(3):
        wmat[piece * ROWS : piece * ROWS + 6, :pixels] = basis
        for ch in range(3):
            wmat[piece * ROWS + 6 + ch, pixels + 128 * ch : pixels + 128 * (ch + 1)] = 1.0
    bas = np.zeros((128, pixels), np.float32)
    bas[:6] = basis
    full = lambda g, *_: (0, 0)
    whole = lambda g, *_: (0, 0, 0)
    image, gtab = pl.pallas_call(
        composite_kernel,
        out_shape=(
            jax.ShapeDtypeStruct((3, tiles, pixels), jnp.float32),
            jax.ShapeDtypeStruct((table_rows, ROWS, 128), jnp.float32),
        ),
        grid_spec=pltpu.PrefetchScalarGridSpec(
            num_scalar_prefetch=2,
            grid=(groups,),
            in_specs=[
                pl.BlockSpec((table_rows, ROWS, 128), whole),
                pl.BlockSpec((1, length, GROUP), lambda g, *_: (g, 0, 0)),
                pl.BlockSpec((3, GROUP, pixels), lambda g, *_: (0, g, 0)),
                pl.BlockSpec(wmat.shape, full),
                pl.BlockSpec(bas.shape, full),
            ],
            out_specs=(
                pl.BlockSpec((3, GROUP, pixels), lambda g, *_: (0, g, 0)),
                pl.BlockSpec((table_rows, ROWS, 128), whole),
            ),
            scratch_shapes=[
                pltpu.VMEM((GROUP, length, length), jnp.bfloat16),
                pltpu.VMEM((GROUP, ROWS, length), jnp.float32),
                pltpu.VMEM((length * GROUP, 128), jnp.float32),
                pltpu.VMEM((length * GROUP, pixels + 3 * 128), jnp.float32),
                pltpu.VMEM((length * GROUP, pixels), jnp.float32),
                pltpu.VMEM((length * GROUP, 128), jnp.float32),
            ],
        ),
        compiler_params=pltpu.CompilerParams(
            dimension_semantics=("arbitrary",), vmem_limit_bytes=60 * 1024 * 1024
        ),
    )(
        slots,
        first_tile,
        table,
        order_cols,
        jnp.transpose(goal, (1, 0, 2)),
        jnp.asarray(wmat, jnp.bfloat16),
        jnp.asarray(bas, jnp.bfloat16),
    )
    return jnp.transpose(image, (1, 0, 2)), gtab


SUB = 8


def project_kernel(params_ref, cam_ref, out_ref):
    @pl.loop(0, params_ref.shape[1] // SUB)
    def _(r):
        part = pl.ds(pl.multiple_of(r * SUB, SUB), SUB)
        gauss = [params_ref[i, part, :] for i in range(params_ref.shape[0])]
        camera = [cam_ref[i * SUB : (i + 1) * SUB, :] for i in range(cam_ref.shape[0] // SUB)]
        for f, value in enumerate(project(gauss, camera)):
            out_ref[f, part, :] = value


def pullback_kernel(params_ref, grads_ref, out_ref):
    views = grads_ref.shape[0]
    depth = params_ref.shape[1]
    cam_base = FIELDS * depth
    cam_n = (grads_ref.shape[1] - cam_base) // SUB

    @pl.loop(0, depth // SUB)
    def _(r):
        part = pl.ds(pl.multiple_of(r * SUB, SUB), SUB)
        gauss = [params_ref[i, part, :] for i in range(params_ref.shape[0])]

        def every_view(values):
            out = []
            for v in range(views):
                camera = [
                    grads_ref[v, cam_base + i * SUB : cam_base + (i + 1) * SUB, :]
                    for i in range(cam_n)
                ]
                out.append(project(values, camera))
            return out

        _, pullback = jax.vjp(every_view, gauss)
        cotangents = [
            [
                grads_ref[v, pl.ds(pl.multiple_of(f * depth + r * SUB, SUB), SUB), :]
                for f in range(FIELDS)
            ]
            for v in range(views)
        ]
        for i, value in enumerate(pullback(cotangents)[0]):
            out_ref[i, part, :] = value


def exchange_kernel(views, mine_ref, out_ref, local_sem, send_sem, recv_sem):
    me = lax.axis_index("view")
    barrier = pltpu.get_barrier_semaphore()
    peers = [lax.rem(me + step, views) for step in range(1, views)]
    for peer in peers:
        pl.semaphore_signal(
            barrier, inc=1, device_id={"view": peer}, device_id_type=pl.DeviceIdType.MESH
        )
    pl.semaphore_wait(barrier, views - 1)
    copies = []
    for step, peer in enumerate(peers):
        copies.append(
            pltpu.make_async_remote_copy(
                src_ref=mine_ref,
                dst_ref=out_ref.at[me],
                send_sem=send_sem.at[step],
                recv_sem=recv_sem.at[step],
                device_id={"view": peer},
                device_id_type=pl.DeviceIdType.MESH,
            )
        )
    for copy in copies:
        copy.start()
    own = pltpu.make_async_copy(mine_ref, out_ref.at[me], local_sem)
    own.start()
    own.wait()
    for copy in copies:
        copy.wait()


def exchange_views(mine):
    views = lax.axis_size("view")
    return pl.pallas_call(
        lambda *refs: exchange_kernel(views, *refs),
        out_shape=jax.ShapeDtypeStruct((views,) + mine.shape, jnp.float32),
        in_specs=[pl.BlockSpec(memory_space=pl.ANY)],
        out_specs=pl.BlockSpec(memory_space=pl.ANY),
        scratch_shapes=[
            pltpu.SemaphoreType.DMA,
            pltpu.SemaphoreType.DMA((views - 1,)),
            pltpu.SemaphoreType.DMA((views - 1,)),
        ],
        compiler_params=pltpu.CompilerParams(collective_id=0, has_side_effects=True),
        name="exchange_views",
    )(mine)


def local(params, camera, targets, send_blocks, tile_blocks, tile_order):
    cells = lax.axis_size("cell")
    cell_index = lax.axis_index("cell")
    values_n, owned = params.shape
    owned_blocks = owned // BLOCK_GAUSSIANS
    per_peer = send_blocks.shape[3]
    slots_n = cells * per_peer
    block_values = FIELDS * BLOCK_GAUSSIANS
    picks = send_blocks[0, 0].reshape(-1)
    depth = owned // 128
    spread = params.reshape(values_n, depth, 128)
    cam_rows = jnp.broadcast_to(
        camera[0][:, None, None], (camera.shape[1], SUB, 128)
    ).reshape(camera.shape[1] * SUB, 128)
    fields = pl.pallas_call(
        project_kernel,
        out_shape=jax.ShapeDtypeStruct((FIELDS, depth, 128), jnp.float32),
        name="project",
    )(spread, cam_rows)
    by_block = jnp.transpose(
        fields.reshape(FIELDS, owned_blocks, BLOCK_GAUSSIANS), (1, 0, 2)
    ).reshape(owned_blocks, block_values)
    chosen = jnp.take(by_block, picks, axis=0).reshape(cells, per_peer * block_values)
    received = lax.all_to_all(chosen, "cell", split_axis=0, concat_axis=0, tiled=True)
    received = received.reshape(slots_n, FIELDS, BLOCK_GAUSSIANS)
    dummy = np.zeros((1, FIELDS, BLOCK_GAUSSIANS), np.float32)
    dummy[:, 5] = -1e30
    table = jnp.concatenate([received, jnp.asarray(dummy)], axis=0)
    table = jnp.tile(
        jnp.pad(table, ((0, 0), (0, ROWS - FIELDS), (0, 0))), (1, 1, 128 // BLOCK_GAUSSIANS)
    )
    blocks = tile_blocks[0]
    slots = jnp.where(blocks < 0, slots_n, blocks)
    first_tile = (cell_index * blocks.shape[0]).astype(jnp.int32).reshape(1)
    picture, gtab = composite(table, slots, tile_order[0], targets[0], first_tile)
    slot_grad = (
        gtab[:slots_n, :FIELDS]
        .reshape(slots_n, FIELDS, 128 // BLOCK_GAUSSIANS, BLOCK_GAUSSIANS)
        .sum(2)
        .reshape(cells, per_peer * block_values)
    )
    returned = lax.all_to_all(slot_grad, "cell", split_axis=0, concat_axis=0, tiled=True)
    chosen_of = (jnp.arange(owned_blocks)[:, None] == picks[None, :]).astype(jnp.float32)
    summed = jnp.dot(
        chosen_of, returned.reshape(slots_n, block_values), precision=HIGHEST_PRECISE
    )
    summed = jnp.transpose(
        summed.reshape(owned_blocks, FIELDS, BLOCK_GAUSSIANS), (1, 0, 2)
    ).reshape(FIELDS * depth, 128)
    by_view = exchange_views(jnp.concatenate([summed, cam_rows], axis=0))
    total = pl.pallas_call(
        pullback_kernel,
        out_shape=jax.ShapeDtypeStruct((values_n, depth, 128), jnp.float32),
        name="pullback",
    )(spread, by_view)
    return (picture[None], total.reshape(values_n, owned))


def solution(mesh):
    return jax.shard_map(
        local,
        mesh=mesh,
        in_specs=(
            P(None, "cell"),
            P("view", None),
            P("view", "cell", None, None),
            P("view", "cell", None, None),
            P("view", "cell", None),
            P("view", "cell", None),
        ),
        out_specs=(P("view", "cell", None, None), P(None, "cell")),
        check_vma=False,
    )
```

```python
import jax
import numpy as np
import jax.numpy as jnp
from jax import lax
from jax.experimental import pallas as pl
from jax.experimental.pallas import tpu as pltpu
from jax.sharding import PartitionSpec as P

BLOCK_GAUSSIANS = 32
TX = 32


HIGHEST_PRECISE = lax.Precision.HIGHEST
SH_ZERO = 0.28209479177387814
SH_ONE = 0.4886025119029199
SH_TWO = [
    1.0925484305920792,
    -1.0925484305920792,
    0.31539156525252005,
    -1.0925484305920792,
    0.5462742152960396,
]
SH_THREE = [
    -0.5900435899266435,
    2.890611442640554,
    -0.4570457994644658,
    0.3731763325901154,
    -0.4570457994644658,
    1.445305721320277,
    -0.5900435899266435,
]


def quat_matrix(qw, qx, qy, qz):
    return [
        [1.0 - 2.0 * (qy * qy + qz * qz), 2.0 * (qx * qy - qw * qz), 2.0 * (qx * qz + qw * qy)],
        [2.0 * (qx * qy + qw * qz), 1.0 - 2.0 * (qx * qx + qz * qz), 2.0 * (qy * qz - qw * qx)],
        [2.0 * (qx * qz - qw * qy), 2.0 * (qy * qz + qw * qx), 1.0 - 2.0 * (qx * qx + qy * qy)],
    ]


def sh_basis(dirx, diry, dirz):
    xx, yy, zz = (dirx * dirx, diry * diry, dirz * dirz)
    return [
        SH_ZERO + 0.0 * dirx,
        -SH_ONE * diry,
        SH_ONE * dirz,
        -SH_ONE * dirx,
        SH_TWO[0] * dirx * diry,
        SH_TWO[1] * diry * dirz,
        SH_TWO[2] * (2.0 * zz - xx - yy),
        SH_TWO[3] * dirx * dirz,
        SH_TWO[4] * (xx - yy),
        SH_THREE[0] * diry * (3.0 * xx - yy),
        SH_THREE[1] * dirx * diry * dirz,
        SH_THREE[2] * diry * (4.0 * zz - xx - yy),
        SH_THREE[3] * dirz * (2.0 * zz - 3.0 * xx - 3.0 * yy),
        SH_THREE[4] * dirx * (4.0 * zz - xx - yy),
        SH_THREE[5] * dirz * (xx - yy),
        SH_THREE[6] * dirx * (xx - 3.0 * yy),
    ]


def project(gauss, camera_row):
    cam_norm = jnp.sqrt(
        camera_row[0] * camera_row[0]
        + camera_row[1] * camera_row[1]
        + camera_row[2] * camera_row[2]
        + camera_row[3] * camera_row[3]
    )
    cam_quat = [camera_row[i] / cam_norm for i in range(4)]
    rotation = quat_matrix(cam_quat[0], cam_quat[1], cam_quat[2], cam_quat[3])
    focal_x, focal_y, centre_x, centre_y = (
        camera_row[7],
        camera_row[8],
        camera_row[9],
        camera_row[10],
    )
    cam_pos = [
        rotation[i][0] * gauss[0]
        + rotation[i][1] * gauss[1]
        + rotation[i][2] * gauss[2]
        + camera_row[4 + i]
        for i in range(3)
    ]
    inverse = 1.0 / cam_pos[2]
    screen_u = focal_x * cam_pos[0] * inverse + centre_x
    screen_w = focal_y * cam_pos[1] * inverse + centre_y
    gauss_norm = jnp.sqrt(
        gauss[6] * gauss[6] + gauss[7] * gauss[7] + gauss[8] * gauss[8] + gauss[9] * gauss[9]
    )
    grot = quat_matrix(
        gauss[6] / gauss_norm, gauss[7] / gauss_norm, gauss[8] / gauss_norm, gauss[9] / gauss_norm
    )
    scales = [jnp.exp(gauss[3 + k]) for k in range(3)]
    axes_cam = [
        [
            rotation[i][0] * grot[0][k] + rotation[i][1] * grot[1][k] + rotation[i][2] * grot[2][k]
            for k in range(3)
        ]
        for i in range(3)
    ]
    row_one = [
        (
            focal_x * inverse * axes_cam[0][k]
            - focal_x * cam_pos[0] * inverse * inverse * axes_cam[2][k]
        )
        * scales[k]
        for k in range(3)
    ]
    row_two = [
        (
            focal_y * inverse * axes_cam[1][k]
            - focal_y * cam_pos[1] * inverse * inverse * axes_cam[2][k]
        )
        * scales[k]
        for k in range(3)
    ]
    entry_a = row_one[0] * row_one[0] + row_one[1] * row_one[1] + row_one[2] * row_one[2] + 0.3
    entry_b = row_one[0] * row_two[0] + row_one[1] * row_two[1] + row_one[2] * row_two[2]
    entry_c = row_two[0] * row_two[0] + row_two[1] * row_two[1] + row_two[2] * row_two[2] + 0.3
    determinant = entry_a * entry_c - entry_b * entry_b
    opacity = -jnp.log(1.0 + jnp.exp(-gauss[10]))
    distance = jnp.sqrt(cam_pos[0] * cam_pos[0] + cam_pos[1] * cam_pos[1] + cam_pos[2] * cam_pos[2])
    direction = [
        (rotation[0][j] * cam_pos[0] + rotation[1][j] * cam_pos[1] + rotation[2][j] * cam_pos[2])
        / distance
        for j in range(3)
    ]
    basis = sh_basis(direction[0], direction[1], direction[2])
    colors = []
    for channel in range(3):
        accum = 0.5 + basis[0] * gauss[11 + channel]
        for order in range(1, 16):
            accum = accum + basis[order] * gauss[11 + 3 * order + channel]
        colors.append(jnp.maximum(accum, 0.0))
    return [
        screen_u,
        screen_w,
        entry_c / determinant,
        -entry_b / determinant,
        entry_a / determinant,
        opacity,
    ] + colors


TILE = 16
GROUP = 8
ROWS = 16
FIELDS = 9
NT_DIMS = (((1,), (1,)), ((), ()))


def pieces3(values):
    one = values.astype(jnp.bfloat16).astype(jnp.float32)
    rest = values - one
    two = rest.astype(jnp.bfloat16).astype(jnp.float32)
    return one, two, rest - two


def basis_rows(pixels):
    ids = np.arange(pixels)
    px = ids % TILE + 0.5 - TILE / 2
    py = ids // TILE + 0.5 - TILE / 2
    return np.stack([np.ones(pixels), px, py, px * px, px * py, py * py]).astype(np.float32)


def composite_kernel(
    slots_ref, first_ref, tab_ref, ord_ref, tgt_ref, wmat_ref, bas_ref, img_ref, gt_ref,
    p_s, f_s, x_s, m_s, w_s, y_s,
):
    group = pl.program_id(0)
    length = ord_ref.shape[1]
    pixels = tgt_ref.shape[2]
    entries = slots_ref.shape[1]
    per = 128 // BLOCK_GAUSSIANS

    @pl.when(group == 0)
    def _():
        gt_ref[...] = jnp.zeros_like(gt_ref)

    lane_part = lax.broadcasted_iota(jnp.int32, (ROWS, 128), 1) // BLOCK_GAUSSIANS
    lane_ids = lax.broadcasted_iota(jnp.int32, (length, length), 1)
    tile0 = first_ref[0] + group * GROUP

    def centre(t):
        tile = tile0 + t
        cx = (lax.rem(tile, TX) * TILE + TILE // 2).astype(jnp.float32)
        cy = (lax.div(tile, TX) * TILE + TILE // 2).astype(jnp.float32)
        return cx, cy

    for t in range(GROUP):
        cols = []
        for v in range(entries // per):
            chunk = None
            for b in range(per):
                block = tab_ref[slots_ref[group * GROUP + t, v * per + b]]
                chunk = block if chunk is None else jnp.where(lane_part == b, block, chunk)
            cols.append(chunk)
        fields = jnp.concatenate(cols, axis=1)
        cx, cy = centre(t)
        u = fields[0:1] - cx
        w = fields[1:2] - cy
        con_a, con_b, con_c, logo = fields[2:3], fields[3:4], fields[4:5], fields[5:6]
        f_s[t] = fields
        coefs = jnp.concatenate(
            [
                logo - 0.5 * (con_a * u * u + con_c * w * w) - con_b * u * w,
                con_a * u + con_b * w,
                con_c * w + con_b * u,
                -0.5 * con_a,
                -con_b,
                -0.5 * con_c,
                fields[6:9],
                jnp.zeros((ROWS - FIELDS, length), jnp.float32),
            ],
            axis=0,
        )
        parts = jnp.concatenate(
            list(pieces3(coefs)) + [jnp.zeros((128 - 3 * ROWS, length), jnp.float32)], axis=0
        ).astype(jnp.bfloat16)
        perm = jnp.where(ord_ref[0, :, t : t + 1] == lane_ids, 1.0, 0.0).astype(jnp.bfloat16)
        p_s[t] = perm
        x_s[pl.ds(t, length, stride=GROUP), :] = lax.dot_general(
            perm, parts, NT_DIMS, preferred_element_type=jnp.float32
        )

    rows = 64 * GROUP
    steps = length * GROUP // rows

    @pl.loop(0, steps)
    def _(c):
        part = pl.ds(pl.multiple_of(c * rows, rows), rows)
        m_s[part, :] = jnp.dot(
            x_s[part, :].astype(jnp.bfloat16), wmat_ref[...], preferred_element_type=jnp.float32
        )

    def twice(x):
        return jnp.concatenate([x] * (pixels // 128), axis=1)

    def load_colors(r):
        return [twice(m_s[r, pixels + 128 * ch : pixels + 128 * (ch + 1)]) for ch in range(3)]

    def forward(k, carry):
        trans, acc = carry
        r = pl.ds(pl.multiple_of(k * GROUP, GROUP), GROUP)
        alpha = jnp.exp(m_s[r, 0:pixels])
        weight = alpha * trans
        m_s[r, 0:pixels] = alpha
        w_s[r, :] = weight
        colors = load_colors(r)
        acc = tuple(a + c * weight for a, c in zip(acc, colors))
        return (trans - weight, acc)

    zero = jnp.zeros((GROUP, pixels), jnp.float32)
    _, image = lax.fori_loop(0, length, forward, (zero + 1.0, (zero, zero, zero)), unroll=8)
    glist = []
    for ch in range(3):
        img_ref[ch] = image[ch]
        glist.append((image[ch] - tgt_ref[ch]) * (1.0 / pixels))

    def backward(i, carry):
        k = length - 1 - i
        r = pl.ds(pl.multiple_of(k * GROUP, GROUP), GROUP)
        alpha = m_s[r, 0:pixels]
        weight = w_s[r, :]
        c = load_colors(r)
        dot = c[0] * glist[0] + c[1] * glist[1] + c[2] * glist[2]
        term = weight * dot
        m_s[r, 0:pixels] = term - carry * (alpha / (1.0 - alpha))
        return carry + term

    lax.fori_loop(0, length, backward, zero, unroll=8)

    grows = jnp.concatenate(
        [jnp.zeros((16, pixels), jnp.float32)]
        + glist
        + [jnp.zeros((128 - 16 - 3 * GROUP, pixels), jnp.float32)],
        axis=0,
    )
    ghigh = grows.astype(jnp.bfloat16)
    glow = (grows - ghigh.astype(jnp.float32)).astype(jnp.bfloat16)

    def nt(a, b):
        return lax.dot_general(a, b, NT_DIMS, preferred_element_type=jnp.float32)

    @pl.loop(0, steps)
    def _(c):
        part = pl.ds(pl.multiple_of(c * rows, rows), rows)
        h = m_s[part, 0:pixels]
        weight = w_s[part, :]
        h1 = h.astype(jnp.bfloat16)
        h2 = (h - h1.astype(jnp.float32)).astype(jnp.bfloat16)
        w1 = weight.astype(jnp.bfloat16)
        w2 = (weight - w1.astype(jnp.float32)).astype(jnp.bfloat16)
        bas = bas_ref[...]
        y_s[part, :] = nt(h1, bas) + nt(h2, bas) + nt(w1, ghigh) + nt(w1, glow) + nt(w2, ghigh)

    used = 16 + 3 * GROUP
    for t in range(GROUP):
        moments = y_s[pl.ds(t, length, stride=GROUP), :].T[0:used]
        stacked = jnp.concatenate(
            list(pieces3(moments)) + [jnp.zeros((128 - 3 * used, length), jnp.float32)], axis=0
        ).astype(jnp.bfloat16)
        back = jnp.dot(stacked, p_s[t], preferred_element_type=jnp.float32)
        back = back[0:used] + back[used : 2 * used] + back[2 * used : 3 * used]
        fields = f_s[t]
        cx, cy = centre(t)
        u = fields[0:1] - cx
        w = fields[1:2] - cy
        con_a, con_b, con_c = fields[2:3], fields[3:4], fields[4:5]
        h0, hx, hy, hxx, hxy, hyy = [back[j : j + 1] for j in range(6)]
        sx = hx - u * h0
        sy = hy - w * h0
        sxx = hxx - 2.0 * u * hx + u * u * h0
        syy = hyy - 2.0 * w * hy + w * w * h0
        sxy = hxy - u * hy - w * hx + u * w * h0
        out = jnp.concatenate(
            [
                con_a * sx + con_b * sy,
                con_c * sy + con_b * sx,
                -0.5 * sxx,
                -sxy,
                -0.5 * syy,
                h0,
            ]
            + [back[16 + ch * GROUP + t : 17 + ch * GROUP + t] for ch in range(3)]
            + [jnp.zeros((ROWS - FIELDS, length), jnp.float32)],
            axis=0,
        )
        for e in range(entries):
            slot = slots_ref[group * GROUP + t, e]
            v, b = divmod(e, per)
            gt_ref[slot] += jnp.where(lane_part == b, out[:, v * 128 : (v + 1) * 128], 0.0)


def composite(table, slots, order, goal, first_tile):
    tiles, length = order.shape
    pixels = goal.shape[-1]
    groups = tiles // GROUP
    table_rows = table.shape[0]
    order_cols = jnp.transpose(order.reshape(groups, GROUP, length), (0, 2, 1))
    basis = basis_rows(pixels)
    wmat = np.zeros((128, pixels + 3 * 128), np.float32)
    for piece in range(3):
        wmat[piece * ROWS : piece * ROWS + 6, :pixels] = basis
        for ch in range(3):
            wmat[piece * ROWS + 6 + ch, pixels + 128 * ch : pixels + 128 * (ch + 1)] = 1.0
    bas = np.zeros((128, pixels), np.float32)
    bas[:6] = basis
    full = lambda g, *_: (0, 0)
    whole = lambda g, *_: (0, 0, 0)
    image, gtab = pl.pallas_call(
        composite_kernel,
        out_shape=(
            jax.ShapeDtypeStruct((3, tiles, pixels), jnp.float32),
            jax.ShapeDtypeStruct((table_rows, ROWS, 128), jnp.float32),
        ),
        grid_spec=pltpu.PrefetchScalarGridSpec(
            num_scalar_prefetch=2,
            grid=(groups,),
            in_specs=[
                pl.BlockSpec((table_rows, ROWS, 128), whole),
                pl.BlockSpec((1, length, GROUP), lambda g, *_: (g, 0, 0)),
                pl.BlockSpec((3, GROUP, pixels), lambda g, *_: (0, g, 0)),
                pl.BlockSpec(wmat.shape, full),
                pl.BlockSpec(bas.shape, full),
            ],
            out_specs=(
                pl.BlockSpec((3, GROUP, pixels), lambda g, *_: (0, g, 0)),
                pl.BlockSpec((table_rows, ROWS, 128), whole),
            ),
            scratch_shapes=[
                pltpu.VMEM((GROUP, length, length), jnp.bfloat16),
                pltpu.VMEM((GROUP, ROWS, length), jnp.float32),
                pltpu.VMEM((length * GROUP, 128), jnp.float32),
                pltpu.VMEM((length * GROUP, pixels + 3 * 128), jnp.float32),
                pltpu.VMEM((length * GROUP, pixels), jnp.float32),
                pltpu.VMEM((length * GROUP, 128), jnp.float32),
            ],
        ),
        compiler_params=pltpu.CompilerParams(
            dimension_semantics=("arbitrary",), vmem_limit_bytes=60 * 1024 * 1024
        ),
    )(
        slots,
        first_tile,
        table,
        order_cols,
        jnp.transpose(goal, (1, 0, 2)),
        jnp.asarray(wmat, jnp.bfloat16),
        jnp.asarray(bas, jnp.bfloat16),
    )
    return jnp.transpose(image, (1, 0, 2)), gtab


SUB = 8


def project_kernel(params_ref, cam_ref, out_ref):
    @pl.loop(0, params_ref.shape[1] // SUB)
    def _(r):
        part = pl.ds(pl.multiple_of(r * SUB, SUB), SUB)
        gauss = [params_ref[i, part, :] for i in range(params_ref.shape[0])]
        camera = [cam_ref[i : i + 1, :] for i in range(cam_ref.shape[0])]
        for f, value in enumerate(project(gauss, camera)):
            out_ref[f, part, :] = value


def pullback_kernel(params_ref, grads_ref, out_ref):
    views = grads_ref.shape[0]
    depth = params_ref.shape[1]
    cam_base = FIELDS * depth

    @pl.loop(0, depth // SUB)
    def _(r):
        part = pl.ds(pl.multiple_of(r * SUB, SUB), SUB)
        gauss = [params_ref[i, part, :] for i in range(params_ref.shape[0])]

        def every_view(values):
            out = []
            for v in range(views):
                camera = [grads_ref[v, i : i + 1, :] for i in range(cam_base, grads_ref.shape[1])]
                out.append(project(values, camera))
            return out

        _, pullback = jax.vjp(every_view, gauss)
        cotangents = [
            [
                grads_ref[v, pl.ds(pl.multiple_of(f * depth + r * SUB, SUB), SUB), :]
                for f in range(FIELDS)
            ]
            for v in range(views)
        ]
        for i, value in enumerate(pullback(cotangents)[0]):
            out_ref[i, part, :] = value


def exchange_kernel(views, mine_ref, out_ref, local_sem, send_sem, recv_sem):
    me = lax.axis_index("view")
    barrier = pltpu.get_barrier_semaphore()
    right, left = lax.rem(me + 1, views), lax.rem(me + views - 1, views)
    half = mine_ref.shape[0] // 2
    parts = [pl.ds(0, half), pl.ds(half, mine_ref.shape[0] - half)]

    def signal(peer):
        pl.semaphore_signal(
            barrier, inc=1, device_id={"view": peer}, device_id_type=pl.DeviceIdType.MESH
        )

    def send(src, owner, part, peer, index):
        copy = pltpu.make_async_remote_copy(
            src_ref=src.at[parts[part]],
            dst_ref=out_ref.at[owner, parts[part]],
            send_sem=send_sem.at[index],
            recv_sem=recv_sem.at[index],
            device_id={"view": peer},
            device_id_type=pl.DeviceIdType.MESH,
        )
        copy.start()
        return copy

    if views == 4:
        signal(right)
        signal(left)
        pl.semaphore_wait(barrier, 2)
        first = send(mine_ref, me, 0, right, 0)
        second = send(mine_ref, me, 1, left, 1)
        copies = [first, second, send(mine_ref, me, 1, right, 2), send(mine_ref, me, 0, left, 3)]
        own = pltpu.make_async_copy(mine_ref, out_ref.at[me], local_sem)
        own.start()
        first.wait_recv()
        copies.append(send(out_ref.at[left], left, 0, right, 4))
        second.wait_recv()
        copies.append(send(out_ref.at[right], right, 1, left, 5))
        first.wait_send()
        second.wait_send()
        for copy in copies[2:]:
            copy.wait()
        own.wait()
        return
    peers = [lax.rem(me + step, views) for step in range(1, views)]
    for peer in peers:
        signal(peer)
    pl.semaphore_wait(barrier, views - 1)
    copies = []
    for step, peer in enumerate(peers):
        copies.append(send(mine_ref, me, 0, peer, 2 * step))
        copies.append(send(mine_ref, me, 1, peer, 2 * step + 1))
    own = pltpu.make_async_copy(mine_ref, out_ref.at[me], local_sem)
    own.start()
    own.wait()
    for copy in copies:
        copy.wait()


def exchange_views(mine):
    views = lax.axis_size("view")
    return pl.pallas_call(
        lambda *refs: exchange_kernel(views, *refs),
        out_shape=jax.ShapeDtypeStruct((views,) + mine.shape, jnp.float32),
        in_specs=[pl.BlockSpec(memory_space=pl.ANY)],
        out_specs=pl.BlockSpec(memory_space=pl.ANY),
        scratch_shapes=[
            pltpu.SemaphoreType.DMA,
            pltpu.SemaphoreType.DMA((2 * views - 2,)),
            pltpu.SemaphoreType.DMA((2 * views - 2,)),
        ],
        compiler_params=pltpu.CompilerParams(collective_id=0, has_side_effects=True),
        name="exchange_views",
    )(mine)


def local(params, camera, targets, send_blocks, tile_blocks, tile_order):
    cells = lax.axis_size("cell")
    cell_index = lax.axis_index("cell")
    values_n, owned = params.shape
    owned_blocks = owned // BLOCK_GAUSSIANS
    per_peer = send_blocks.shape[3]
    slots_n = cells * per_peer
    block_values = FIELDS * BLOCK_GAUSSIANS
    picks = send_blocks[0, 0].reshape(-1)
    depth = owned // 128
    spread = params.reshape(values_n, depth, 128)
    cam_rows = jnp.broadcast_to(
        jnp.pad(camera[0], (0, -camera.shape[1] % SUB))[:, None],
        (camera.shape[1] + -camera.shape[1] % SUB, 128),
    )
    fields = pl.pallas_call(
        project_kernel,
        out_shape=jax.ShapeDtypeStruct((FIELDS, depth, 128), jnp.float32),
        name="project",
    )(spread, cam_rows)
    by_block = jnp.transpose(
        fields.reshape(FIELDS, owned_blocks, BLOCK_GAUSSIANS), (1, 0, 2)
    ).reshape(owned_blocks, block_values)
    chosen = jnp.take(by_block, picks, axis=0).reshape(cells, per_peer * block_values)
    received = lax.all_to_all(chosen, "cell", split_axis=0, concat_axis=0, tiled=True)
    received = received.reshape(slots_n, FIELDS, BLOCK_GAUSSIANS)
    dummy = np.zeros((1, FIELDS, BLOCK_GAUSSIANS), np.float32)
    dummy[:, 5] = -1e30
    table = jnp.concatenate([received, jnp.asarray(dummy)], axis=0)
    table = jnp.tile(
        jnp.pad(table, ((0, 0), (0, ROWS - FIELDS), (0, 0))), (1, 1, 128 // BLOCK_GAUSSIANS)
    )
    blocks = tile_blocks[0]
    slots = jnp.where(blocks < 0, slots_n, blocks)
    first_tile = (cell_index * blocks.shape[0]).astype(jnp.int32).reshape(1)
    picture, gtab = composite(table, slots, tile_order[0], targets[0], first_tile)
    slot_grad = (
        gtab[:slots_n, :FIELDS]
        .reshape(slots_n, FIELDS, 128 // BLOCK_GAUSSIANS, BLOCK_GAUSSIANS)
        .sum(2)
        .reshape(cells, per_peer * block_values)
    )
    returned = lax.all_to_all(slot_grad, "cell", split_axis=0, concat_axis=0, tiled=True)
    chosen_of = (jnp.arange(owned_blocks)[:, None] == picks[None, :]).astype(jnp.float32)
    summed = jnp.dot(
        chosen_of, returned.reshape(slots_n, block_values), precision=HIGHEST_PRECISE
    )
    summed = jnp.transpose(
        summed.reshape(owned_blocks, FIELDS, BLOCK_GAUSSIANS), (1, 0, 2)
    ).reshape(FIELDS * depth, 128)
    by_view = exchange_views(jnp.concatenate([summed, cam_rows], axis=0))
    total = pl.pallas_call(
        pullback_kernel,
        out_shape=jax.ShapeDtypeStruct((values_n, depth, 128), jnp.float32),
        name="pullback",
    )(spread, by_view)
    return (picture[None], total.reshape(values_n, owned))


def solution(mesh):
    return jax.shard_map(
        local,
        mesh=mesh,
        in_specs=(
            P(None, "cell"),
            P("view", None),
            P("view", "cell", None, None),
            P("view", "cell", None, None),
            P("view", "cell", None),
            P("view", "cell", None),
        ),
        out_specs=(P("view", "cell", None, None), P(None, "cell")),
        check_vma=False,
    )
```

```python
import jax
import numpy as np
import jax.numpy as jnp
from jax import lax
from jax.experimental import pallas as pl
from jax.experimental.pallas import tpu as pltpu
from jax.sharding import PartitionSpec as P

BLOCK_GAUSSIANS = 32
TX = 32


HIGHEST_PRECISE = lax.Precision.HIGHEST
SH_ZERO = 0.28209479177387814
SH_ONE = 0.4886025119029199
SH_TWO = [
    1.0925484305920792,
    -1.0925484305920792,
    0.31539156525252005,
    -1.0925484305920792,
    0.5462742152960396,
]
SH_THREE = [
    -0.5900435899266435,
    2.890611442640554,
    -0.4570457994644658,
    0.3731763325901154,
    -0.4570457994644658,
    1.445305721320277,
    -0.5900435899266435,
]


def quat_matrix(qw, qx, qy, qz):
    return [
        [1.0 - 2.0 * (qy * qy + qz * qz), 2.0 * (qx * qy - qw * qz), 2.0 * (qx * qz + qw * qy)],
        [2.0 * (qx * qy + qw * qz), 1.0 - 2.0 * (qx * qx + qz * qz), 2.0 * (qy * qz - qw * qx)],
        [2.0 * (qx * qz - qw * qy), 2.0 * (qy * qz + qw * qx), 1.0 - 2.0 * (qx * qx + qy * qy)],
    ]


def sh_basis(dirx, diry, dirz):
    xx, yy, zz = (dirx * dirx, diry * diry, dirz * dirz)
    return [
        SH_ZERO + 0.0 * dirx,
        -SH_ONE * diry,
        SH_ONE * dirz,
        -SH_ONE * dirx,
        SH_TWO[0] * dirx * diry,
        SH_TWO[1] * diry * dirz,
        SH_TWO[2] * (2.0 * zz - xx - yy),
        SH_TWO[3] * dirx * dirz,
        SH_TWO[4] * (xx - yy),
        SH_THREE[0] * diry * (3.0 * xx - yy),
        SH_THREE[1] * dirx * diry * dirz,
        SH_THREE[2] * diry * (4.0 * zz - xx - yy),
        SH_THREE[3] * dirz * (2.0 * zz - 3.0 * xx - 3.0 * yy),
        SH_THREE[4] * dirx * (4.0 * zz - xx - yy),
        SH_THREE[5] * dirz * (xx - yy),
        SH_THREE[6] * dirx * (xx - 3.0 * yy),
    ]


def project(gauss, camera_row):
    cam_norm = jnp.sqrt(
        camera_row[0] * camera_row[0]
        + camera_row[1] * camera_row[1]
        + camera_row[2] * camera_row[2]
        + camera_row[3] * camera_row[3]
    )
    cam_quat = [camera_row[i] / cam_norm for i in range(4)]
    rotation = quat_matrix(cam_quat[0], cam_quat[1], cam_quat[2], cam_quat[3])
    focal_x, focal_y, centre_x, centre_y = (
        camera_row[7],
        camera_row[8],
        camera_row[9],
        camera_row[10],
    )
    cam_pos = [
        rotation[i][0] * gauss[0]
        + rotation[i][1] * gauss[1]
        + rotation[i][2] * gauss[2]
        + camera_row[4 + i]
        for i in range(3)
    ]
    inverse = 1.0 / cam_pos[2]
    screen_u = focal_x * cam_pos[0] * inverse + centre_x
    screen_w = focal_y * cam_pos[1] * inverse + centre_y
    gauss_norm = jnp.sqrt(
        gauss[6] * gauss[6] + gauss[7] * gauss[7] + gauss[8] * gauss[8] + gauss[9] * gauss[9]
    )
    grot = quat_matrix(
        gauss[6] / gauss_norm, gauss[7] / gauss_norm, gauss[8] / gauss_norm, gauss[9] / gauss_norm
    )
    scales = [jnp.exp(gauss[3 + k]) for k in range(3)]
    axes_cam = [
        [
            rotation[i][0] * grot[0][k] + rotation[i][1] * grot[1][k] + rotation[i][2] * grot[2][k]
            for k in range(3)
        ]
        for i in range(3)
    ]
    row_one = [
        (
            focal_x * inverse * axes_cam[0][k]
            - focal_x * cam_pos[0] * inverse * inverse * axes_cam[2][k]
        )
        * scales[k]
        for k in range(3)
    ]
    row_two = [
        (
            focal_y * inverse * axes_cam[1][k]
            - focal_y * cam_pos[1] * inverse * inverse * axes_cam[2][k]
        )
        * scales[k]
        for k in range(3)
    ]
    entry_a = row_one[0] * row_one[0] + row_one[1] * row_one[1] + row_one[2] * row_one[2] + 0.3
    entry_b = row_one[0] * row_two[0] + row_one[1] * row_two[1] + row_one[2] * row_two[2]
    entry_c = row_two[0] * row_two[0] + row_two[1] * row_two[1] + row_two[2] * row_two[2] + 0.3
    determinant = entry_a * entry_c - entry_b * entry_b
    opacity = -jnp.log(1.0 + jnp.exp(-gauss[10]))
    distance = jnp.sqrt(cam_pos[0] * cam_pos[0] + cam_pos[1] * cam_pos[1] + cam_pos[2] * cam_pos[2])
    direction = [
        (rotation[0][j] * cam_pos[0] + rotation[1][j] * cam_pos[1] + rotation[2][j] * cam_pos[2])
        / distance
        for j in range(3)
    ]
    basis = sh_basis(direction[0], direction[1], direction[2])
    colors = []
    for channel in range(3):
        accum = 0.5 + basis[0] * gauss[11 + channel]
        for order in range(1, 16):
            accum = accum + basis[order] * gauss[11 + 3 * order + channel]
        colors.append(jnp.maximum(accum, 0.0))
    return [
        screen_u,
        screen_w,
        entry_c / determinant,
        -entry_b / determinant,
        entry_a / determinant,
        opacity,
    ] + colors


TILE = 16
GROUP = 8
ROWS = 16
FIELDS = 9
NT_DIMS = (((1,), (1,)), ((), ()))


def pieces3(values):
    one = values.astype(jnp.bfloat16).astype(jnp.float32)
    rest = values - one
    two = rest.astype(jnp.bfloat16).astype(jnp.float32)
    return one, two, rest - two


def basis_rows(pixels):
    ids = np.arange(pixels)
    px = ids % TILE + 0.5 - TILE / 2
    py = ids // TILE + 0.5 - TILE / 2
    return np.stack([np.ones(pixels), px, py, px * px, px * py, py * py]).astype(np.float32)


def composite_kernel(
    slots_ref, first_ref, tab_ref, ord_ref, tgt_ref, wmat_ref, bas_ref, img_ref, gt_ref,
    p_s, f_s, x_s, m_s, w_s, y_s,
):
    group = pl.program_id(0)
    length = ord_ref.shape[1]
    pixels = tgt_ref.shape[2]
    entries = slots_ref.shape[1]
    per = 128 // BLOCK_GAUSSIANS

    @pl.when(group == 0)
    def _():
        gt_ref[...] = jnp.zeros_like(gt_ref)

    lane_part = lax.broadcasted_iota(jnp.int32, (ROWS, 128), 1) // BLOCK_GAUSSIANS
    lane_ids = lax.broadcasted_iota(jnp.int32, (length, length), 1)
    tile0 = first_ref[0] + group * GROUP

    def centre(t):
        tile = tile0 + t
        cx = (lax.rem(tile, TX) * TILE + TILE // 2).astype(jnp.float32)
        cy = (lax.div(tile, TX) * TILE + TILE // 2).astype(jnp.float32)
        return cx, cy

    for t in range(GROUP):
        cols = []
        for v in range(entries // per):
            chunk = None
            for b in range(per):
                block = tab_ref[slots_ref[group * GROUP + t, v * per + b]]
                chunk = block if chunk is None else jnp.where(lane_part == b, block, chunk)
            cols.append(chunk)
        fields = jnp.concatenate(cols, axis=1)
        cx, cy = centre(t)
        u = fields[0:1] - cx
        w = fields[1:2] - cy
        con_a, con_b, con_c, logo = fields[2:3], fields[3:4], fields[4:5], fields[5:6]
        f_s[t] = fields
        coefs = jnp.concatenate(
            [
                logo - 0.5 * (con_a * u * u + con_c * w * w) - con_b * u * w,
                con_a * u + con_b * w,
                con_c * w + con_b * u,
                -0.5 * con_a,
                -con_b,
                -0.5 * con_c,
                fields[6:9],
                jnp.zeros((ROWS - FIELDS, length), jnp.float32),
            ],
            axis=0,
        )
        parts = jnp.concatenate(
            list(pieces3(coefs)) + [jnp.zeros((128 - 3 * ROWS, length), jnp.float32)], axis=0
        ).astype(jnp.bfloat16)
        perm = jnp.where(ord_ref[0, :, t : t + 1] == lane_ids, 1.0, 0.0).astype(jnp.bfloat16)
        p_s[t] = perm
        x_s[pl.ds(t, length, stride=GROUP), :] = lax.dot_general(
            perm, parts, NT_DIMS, preferred_element_type=jnp.float32
        )

    rows = 64 * GROUP
    steps = length * GROUP // rows

    @pl.loop(0, steps)
    def _(c):
        part = pl.ds(pl.multiple_of(c * rows, rows), rows)
        m_s[part, :] = jnp.dot(
            x_s[part, :].astype(jnp.bfloat16), wmat_ref[...], preferred_element_type=jnp.float32
        )

    def twice(x):
        return jnp.concatenate([x] * (pixels // 128), axis=1)

    def load_colors(r):
        return [twice(m_s[r, pixels + 128 * ch : pixels + 128 * (ch + 1)]) for ch in range(3)]

    def forward(k, carry):
        trans, acc = carry
        r = pl.ds(pl.multiple_of(k * GROUP, GROUP), GROUP)
        alpha = jnp.exp(m_s[r, 0:pixels])
        weight = alpha * trans
        m_s[r, 0:pixels] = alpha
        w_s[r, :] = weight
        colors = load_colors(r)
        acc = tuple(a + c * weight for a, c in zip(acc, colors))
        return (trans - weight, acc)

    zero = jnp.zeros((GROUP, pixels), jnp.float32)
    _, image = lax.fori_loop(0, length, forward, (zero + 1.0, (zero, zero, zero)), unroll=16)
    glist = []
    for ch in range(3):
        img_ref[ch] = image[ch]
        glist.append((image[ch] - tgt_ref[ch]) * (1.0 / pixels))

    def backward(i, behind):
        k = length - 1 - i
        r = pl.ds(pl.multiple_of(k * GROUP, GROUP), GROUP)
        c = load_colors(r)
        delta = (c[0] * glist[0] + c[1] * glist[1] + c[2] * glist[2]) - behind
        alpha = m_s[r, 0:pixels]
        m_s[r, 0:pixels] = w_s[r, :] * delta
        return behind + alpha * delta

    lax.fori_loop(0, length, backward, zero, unroll=16)

    grows = jnp.concatenate(
        [jnp.zeros((16, pixels), jnp.float32)]
        + glist
        + [jnp.zeros((128 - 16 - 3 * GROUP, pixels), jnp.float32)],
        axis=0,
    )
    ghigh = grows.astype(jnp.bfloat16)
    glow = (grows - ghigh.astype(jnp.float32)).astype(jnp.bfloat16)
    gboth = jnp.concatenate([ghigh, glow], axis=0)

    def nt(a, b):
        return lax.dot_general(a, b, NT_DIMS, preferred_element_type=jnp.float32)

    @pl.loop(0, steps)
    def _(c):
        part = pl.ds(pl.multiple_of(c * rows, rows), rows)
        h = m_s[part, 0:pixels]
        weight = w_s[part, :]
        h1 = h.astype(jnp.bfloat16)
        h2 = (h - h1.astype(jnp.float32)).astype(jnp.bfloat16)
        w1 = weight.astype(jnp.bfloat16)
        w2 = (weight - w1.astype(jnp.float32)).astype(jnp.bfloat16)
        bas = bas_ref[...]
        both = nt(w1, gboth)
        y_s[part, :] = (
            nt(h1, bas) + nt(h2, bas) + nt(w2, ghigh) + both[:, 0:128] + both[:, 128:256]
        )

    used = 16 + 3 * GROUP
    for t in range(GROUP):
        moments = y_s[pl.ds(t, length, stride=GROUP), :].T[0:used]
        stacked = jnp.concatenate(
            list(pieces3(moments)) + [jnp.zeros((128 - 3 * used, length), jnp.float32)], axis=0
        ).astype(jnp.bfloat16)
        back = jnp.dot(stacked, p_s[t], preferred_element_type=jnp.float32)
        back = back[0:used] + back[used : 2 * used] + back[2 * used : 3 * used]
        fields = f_s[t]
        cx, cy = centre(t)
        u = fields[0:1] - cx
        w = fields[1:2] - cy
        con_a, con_b, con_c = fields[2:3], fields[3:4], fields[4:5]
        h0, hx, hy, hxx, hxy, hyy = [back[j : j + 1] for j in range(6)]
        sx = hx - u * h0
        sy = hy - w * h0
        sxx = hxx - 2.0 * u * hx + u * u * h0
        syy = hyy - 2.0 * w * hy + w * w * h0
        sxy = hxy - u * hy - w * hx + u * w * h0
        out = jnp.concatenate(
            [
                con_a * sx + con_b * sy,
                con_c * sy + con_b * sx,
                -0.5 * sxx,
                -sxy,
                -0.5 * syy,
                h0,
            ]
            + [back[16 + ch * GROUP + t : 17 + ch * GROUP + t] for ch in range(3)]
            + [jnp.zeros((ROWS - FIELDS, length), jnp.float32)],
            axis=0,
        )
        for e in range(entries):
            slot = slots_ref[group * GROUP + t, e]
            v, b = divmod(e, per)
            gt_ref[slot] += jnp.where(lane_part == b, out[:, v * 128 : (v + 1) * 128], 0.0)


def composite(table, slots, order, goal, first_tile):
    tiles, length = order.shape
    pixels = goal.shape[-1]
    groups = tiles // GROUP
    table_rows = table.shape[0]
    order_cols = jnp.transpose(order.reshape(groups, GROUP, length), (0, 2, 1))
    basis = basis_rows(pixels)
    wmat = np.zeros((128, pixels + 3 * 128), np.float32)
    for piece in range(3):
        wmat[piece * ROWS : piece * ROWS + 6, :pixels] = basis
        for ch in range(3):
            wmat[piece * ROWS + 6 + ch, pixels + 128 * ch : pixels + 128 * (ch + 1)] = 1.0
    bas = np.zeros((128, pixels), np.float32)
    bas[:6] = basis
    full = lambda g, *_: (0, 0)
    whole = lambda g, *_: (0, 0, 0)
    image, gtab = pl.pallas_call(
        composite_kernel,
        out_shape=(
            jax.ShapeDtypeStruct((3, tiles, pixels), jnp.float32),
            jax.ShapeDtypeStruct((table_rows, ROWS, 128), jnp.float32),
        ),
        grid_spec=pltpu.PrefetchScalarGridSpec(
            num_scalar_prefetch=2,
            grid=(groups,),
            in_specs=[
                pl.BlockSpec((table_rows, ROWS, 128), whole),
                pl.BlockSpec((1, length, GROUP), lambda g, *_: (g, 0, 0)),
                pl.BlockSpec((3, GROUP, pixels), lambda g, *_: (0, g, 0)),
                pl.BlockSpec(wmat.shape, full),
                pl.BlockSpec(bas.shape, full),
            ],
            out_specs=(
                pl.BlockSpec((3, GROUP, pixels), lambda g, *_: (0, g, 0)),
                pl.BlockSpec((table_rows, ROWS, 128), whole),
            ),
            scratch_shapes=[
                pltpu.VMEM((GROUP, length, length), jnp.bfloat16),
                pltpu.VMEM((GROUP, ROWS, length), jnp.float32),
                pltpu.VMEM((length * GROUP, 128), jnp.float32),
                pltpu.VMEM((length * GROUP, pixels + 3 * 128), jnp.float32),
                pltpu.VMEM((length * GROUP, pixels), jnp.float32),
                pltpu.VMEM((length * GROUP, 128), jnp.float32),
            ],
        ),
        compiler_params=pltpu.CompilerParams(
            dimension_semantics=("arbitrary",), vmem_limit_bytes=60 * 1024 * 1024
        ),
    )(
        slots,
        first_tile,
        table,
        order_cols,
        jnp.transpose(goal, (1, 0, 2)),
        jnp.asarray(wmat, jnp.bfloat16),
        jnp.asarray(bas, jnp.bfloat16),
    )
    return jnp.transpose(image, (1, 0, 2)), gtab


SUB = 8


def project_kernel(params_ref, cam_ref, out_ref):
    @pl.loop(0, params_ref.shape[1] // SUB)
    def _(r):
        part = pl.ds(pl.multiple_of(r * SUB, SUB), SUB)
        gauss = [params_ref[i, part, :] for i in range(params_ref.shape[0])]
        camera = [cam_ref[i : i + 1, :] for i in range(cam_ref.shape[0])]
        for f, value in enumerate(project(gauss, camera)):
            out_ref[f, part, :] = value


def pullback_kernel(params_ref, grads_ref, out_ref):
    views = grads_ref.shape[0]
    depth = params_ref.shape[1]
    cam_base = FIELDS * depth

    @pl.loop(0, depth // SUB)
    def _(r):
        part = pl.ds(pl.multiple_of(r * SUB, SUB), SUB)
        gauss = [params_ref[i, part, :] for i in range(params_ref.shape[0])]

        def every_view(values):
            out = []
            for v in range(views):
                camera = [grads_ref[v, i : i + 1, :] for i in range(cam_base, grads_ref.shape[1])]
                out.append(project(values, camera))
            return out

        _, pullback = jax.vjp(every_view, gauss)
        cotangents = [
            [
                grads_ref[v, pl.ds(pl.multiple_of(f * depth + r * SUB, SUB), SUB), :]
                for f in range(FIELDS)
            ]
            for v in range(views)
        ]
        for i, value in enumerate(pullback(cotangents)[0]):
            out_ref[i, part, :] = value


def exchange_kernel(views, mine_ref, out_ref, local_sem, send_sem, recv_sem):
    me = lax.axis_index("view")
    barrier = pltpu.get_barrier_semaphore()
    right, left = lax.rem(me + 1, views), lax.rem(me + views - 1, views)
    half = mine_ref.shape[0] // 2
    parts = [pl.ds(0, half), pl.ds(half, mine_ref.shape[0] - half)]

    def signal(peer):
        pl.semaphore_signal(
            barrier, inc=1, device_id={"view": peer}, device_id_type=pl.DeviceIdType.MESH
        )

    def send(src, owner, part, peer, index):
        copy = pltpu.make_async_remote_copy(
            src_ref=src.at[parts[part]],
            dst_ref=out_ref.at[owner, parts[part]],
            send_sem=send_sem.at[index],
            recv_sem=recv_sem.at[index],
            device_id={"view": peer},
            device_id_type=pl.DeviceIdType.MESH,
        )
        copy.start()
        return copy

    if views == 4:
        signal(right)
        signal(left)
        pl.semaphore_wait(barrier, 2)
        first = send(mine_ref, me, 0, right, 0)
        second = send(mine_ref, me, 1, left, 1)
        copies = [first, second, send(mine_ref, me, 1, right, 2), send(mine_ref, me, 0, left, 3)]
        own = pltpu.make_async_copy(mine_ref, out_ref.at[me], local_sem)
        own.start()
        first.wait_recv()
        copies.append(send(out_ref.at[left], left, 0, right, 4))
        second.wait_recv()
        copies.append(send(out_ref.at[right], right, 1, left, 5))
        first.wait_send()
        second.wait_send()
        for copy in copies[2:]:
            copy.wait()
        own.wait()
        return
    peers = [lax.rem(me + step, views) for step in range(1, views)]
    for peer in peers:
        signal(peer)
    pl.semaphore_wait(barrier, views - 1)
    copies = []
    for step, peer in enumerate(peers):
        copies.append(send(mine_ref, me, 0, peer, 2 * step))
        copies.append(send(mine_ref, me, 1, peer, 2 * step + 1))
    own = pltpu.make_async_copy(mine_ref, out_ref.at[me], local_sem)
    own.start()
    own.wait()
    for copy in copies:
        copy.wait()


def exchange_views(mine):
    views = lax.axis_size("view")
    return pl.pallas_call(
        lambda *refs: exchange_kernel(views, *refs),
        out_shape=jax.ShapeDtypeStruct((views,) + mine.shape, jnp.float32),
        in_specs=[pl.BlockSpec(memory_space=pl.ANY)],
        out_specs=pl.BlockSpec(memory_space=pl.ANY),
        scratch_shapes=[
            pltpu.SemaphoreType.DMA,
            pltpu.SemaphoreType.DMA((2 * views - 2,)),
            pltpu.SemaphoreType.DMA((2 * views - 2,)),
        ],
        compiler_params=pltpu.CompilerParams(collective_id=0, has_side_effects=True),
        name="exchange_views",
    )(mine)


def local(params, camera, targets, send_blocks, tile_blocks, tile_order):
    cells = lax.axis_size("cell")
    cell_index = lax.axis_index("cell")
    values_n, owned = params.shape
    owned_blocks = owned // BLOCK_GAUSSIANS
    per_peer = send_blocks.shape[3]
    slots_n = cells * per_peer
    block_values = FIELDS * BLOCK_GAUSSIANS
    picks = send_blocks[0, 0].reshape(-1)
    depth = owned // 128
    spread = params.reshape(values_n, depth, 128)
    cam_rows = jnp.broadcast_to(
        jnp.pad(camera[0], (0, -camera.shape[1] % SUB))[:, None],
        (camera.shape[1] + -camera.shape[1] % SUB, 128),
    )
    fields = pl.pallas_call(
        project_kernel,
        out_shape=jax.ShapeDtypeStruct((FIELDS, depth, 128), jnp.float32),
        name="project",
    )(spread, cam_rows)
    by_block = jnp.transpose(
        fields.reshape(FIELDS, owned_blocks, BLOCK_GAUSSIANS), (1, 0, 2)
    ).reshape(owned_blocks, block_values)
    chosen = jnp.take(by_block, picks, axis=0).reshape(cells, per_peer * block_values)
    received = lax.all_to_all(chosen, "cell", split_axis=0, concat_axis=0, tiled=True)
    received = received.reshape(slots_n, FIELDS, BLOCK_GAUSSIANS)
    dummy = np.zeros((1, FIELDS, BLOCK_GAUSSIANS), np.float32)
    dummy[:, 5] = -1e30
    table = jnp.concatenate([received, jnp.asarray(dummy)], axis=0)
    table = jnp.tile(
        jnp.pad(table, ((0, 0), (0, ROWS - FIELDS), (0, 0))), (1, 1, 128 // BLOCK_GAUSSIANS)
    )
    blocks = tile_blocks[0]
    slots = jnp.where(blocks < 0, slots_n, blocks)
    first_tile = (cell_index * blocks.shape[0]).astype(jnp.int32).reshape(1)
    picture, gtab = composite(table, slots, tile_order[0], targets[0], first_tile)
    slot_grad = (
        gtab[:slots_n, :FIELDS]
        .reshape(slots_n, FIELDS, 128 // BLOCK_GAUSSIANS, BLOCK_GAUSSIANS)
        .sum(2)
        .reshape(cells, per_peer * block_values)
    )
    returned = lax.all_to_all(slot_grad, "cell", split_axis=0, concat_axis=0, tiled=True)
    chosen_of = (jnp.arange(owned_blocks)[:, None] == picks[None, :]).astype(jnp.float32)
    summed = jnp.dot(
        chosen_of, returned.reshape(slots_n, block_values), precision=HIGHEST_PRECISE
    )
    summed = jnp.transpose(
        summed.reshape(owned_blocks, FIELDS, BLOCK_GAUSSIANS), (1, 0, 2)
    ).reshape(FIELDS * depth, 128)
    by_view = exchange_views(jnp.concatenate([summed, cam_rows], axis=0))
    total = pl.pallas_call(
        pullback_kernel,
        out_shape=jax.ShapeDtypeStruct((values_n, depth, 128), jnp.float32),
        name="pullback",
    )(spread, by_view)
    return (picture[None], total.reshape(values_n, owned))


def solution(mesh):
    return jax.shard_map(
        local,
        mesh=mesh,
        in_specs=(
            P(None, "cell"),
            P("view", None),
            P("view", "cell", None, None),
            P("view", "cell", None, None),
            P("view", "cell", None),
            P("view", "cell", None),
        ),
        out_specs=(P("view", "cell", None, None), P(None, "cell")),
        check_vma=False,
    )
```

```python
import jax
import numpy as np
import jax.numpy as jnp
from jax import lax
from jax.experimental import pallas as pl
from jax.experimental.pallas import tpu as pltpu
from jax.sharding import PartitionSpec as P

BLOCK_GAUSSIANS = 32
TX = 32


HIGHEST_PRECISE = lax.Precision.HIGHEST
SH_ZERO = 0.28209479177387814
SH_ONE = 0.4886025119029199
SH_TWO = [
    1.0925484305920792,
    -1.0925484305920792,
    0.31539156525252005,
    -1.0925484305920792,
    0.5462742152960396,
]
SH_THREE = [
    -0.5900435899266435,
    2.890611442640554,
    -0.4570457994644658,
    0.3731763325901154,
    -0.4570457994644658,
    1.445305721320277,
    -0.5900435899266435,
]


def quat_matrix(qw, qx, qy, qz):
    return [
        [1.0 - 2.0 * (qy * qy + qz * qz), 2.0 * (qx * qy - qw * qz), 2.0 * (qx * qz + qw * qy)],
        [2.0 * (qx * qy + qw * qz), 1.0 - 2.0 * (qx * qx + qz * qz), 2.0 * (qy * qz - qw * qx)],
        [2.0 * (qx * qz - qw * qy), 2.0 * (qy * qz + qw * qx), 1.0 - 2.0 * (qx * qx + qy * qy)],
    ]


def sh_basis(dirx, diry, dirz):
    xx, yy, zz = (dirx * dirx, diry * diry, dirz * dirz)
    return [
        SH_ZERO + 0.0 * dirx,
        -SH_ONE * diry,
        SH_ONE * dirz,
        -SH_ONE * dirx,
        SH_TWO[0] * dirx * diry,
        SH_TWO[1] * diry * dirz,
        SH_TWO[2] * (2.0 * zz - xx - yy),
        SH_TWO[3] * dirx * dirz,
        SH_TWO[4] * (xx - yy),
        SH_THREE[0] * diry * (3.0 * xx - yy),
        SH_THREE[1] * dirx * diry * dirz,
        SH_THREE[2] * diry * (4.0 * zz - xx - yy),
        SH_THREE[3] * dirz * (2.0 * zz - 3.0 * xx - 3.0 * yy),
        SH_THREE[4] * dirx * (4.0 * zz - xx - yy),
        SH_THREE[5] * dirz * (xx - yy),
        SH_THREE[6] * dirx * (xx - 3.0 * yy),
    ]


def project(gauss, camera_row):
    cam_norm = jnp.sqrt(
        camera_row[0] * camera_row[0]
        + camera_row[1] * camera_row[1]
        + camera_row[2] * camera_row[2]
        + camera_row[3] * camera_row[3]
    )
    cam_quat = [camera_row[i] / cam_norm for i in range(4)]
    rotation = quat_matrix(cam_quat[0], cam_quat[1], cam_quat[2], cam_quat[3])
    focal_x, focal_y, centre_x, centre_y = (
        camera_row[7],
        camera_row[8],
        camera_row[9],
        camera_row[10],
    )
    cam_pos = [
        rotation[i][0] * gauss[0]
        + rotation[i][1] * gauss[1]
        + rotation[i][2] * gauss[2]
        + camera_row[4 + i]
        for i in range(3)
    ]
    inverse = 1.0 / cam_pos[2]
    screen_u = focal_x * cam_pos[0] * inverse + centre_x
    screen_w = focal_y * cam_pos[1] * inverse + centre_y
    gauss_norm = jnp.sqrt(
        gauss[6] * gauss[6] + gauss[7] * gauss[7] + gauss[8] * gauss[8] + gauss[9] * gauss[9]
    )
    grot = quat_matrix(
        gauss[6] / gauss_norm, gauss[7] / gauss_norm, gauss[8] / gauss_norm, gauss[9] / gauss_norm
    )
    scales = [jnp.exp(gauss[3 + k]) for k in range(3)]
    axes_cam = [
        [
            rotation[i][0] * grot[0][k] + rotation[i][1] * grot[1][k] + rotation[i][2] * grot[2][k]
            for k in range(3)
        ]
        for i in range(3)
    ]
    row_one = [
        (
            focal_x * inverse * axes_cam[0][k]
            - focal_x * cam_pos[0] * inverse * inverse * axes_cam[2][k]
        )
        * scales[k]
        for k in range(3)
    ]
    row_two = [
        (
            focal_y * inverse * axes_cam[1][k]
            - focal_y * cam_pos[1] * inverse * inverse * axes_cam[2][k]
        )
        * scales[k]
        for k in range(3)
    ]
    entry_a = row_one[0] * row_one[0] + row_one[1] * row_one[1] + row_one[2] * row_one[2] + 0.3
    entry_b = row_one[0] * row_two[0] + row_one[1] * row_two[1] + row_one[2] * row_two[2]
    entry_c = row_two[0] * row_two[0] + row_two[1] * row_two[1] + row_two[2] * row_two[2] + 0.3
    determinant = entry_a * entry_c - entry_b * entry_b
    opacity = -jnp.log(1.0 + jnp.exp(-gauss[10]))
    distance = jnp.sqrt(cam_pos[0] * cam_pos[0] + cam_pos[1] * cam_pos[1] + cam_pos[2] * cam_pos[2])
    direction = [
        (rotation[0][j] * cam_pos[0] + rotation[1][j] * cam_pos[1] + rotation[2][j] * cam_pos[2])
        / distance
        for j in range(3)
    ]
    basis = sh_basis(direction[0], direction[1], direction[2])
    colors = []
    for channel in range(3):
        accum = 0.5 + basis[0] * gauss[11 + channel]
        for order in range(1, 16):
            accum = accum + basis[order] * gauss[11 + 3 * order + channel]
        colors.append(jnp.maximum(accum, 0.0))
    return [
        screen_u,
        screen_w,
        entry_c / determinant,
        -entry_b / determinant,
        entry_a / determinant,
        opacity,
    ] + colors


TILE = 16
GROUP = 8
ROWS = 16
FIELDS = 9
NT_DIMS = (((1,), (1,)), ((), ()))


def pieces3(values):
    one = values.astype(jnp.bfloat16).astype(jnp.float32)
    rest = values - one
    two = rest.astype(jnp.bfloat16).astype(jnp.float32)
    return one, two, rest - two


def basis_rows(pixels):
    ids = np.arange(pixels)
    px = ids % TILE + 0.5 - TILE / 2
    py = ids // TILE + 0.5 - TILE / 2
    return np.stack([np.ones(pixels), px, py, px * px, px * py, py * py]).astype(np.float32)


def composite_kernel(
    slots_ref, first_ref, tab_ref, ord_ref, tgt_ref, wmat_ref, bas_ref, img_ref, gt_ref,
    p_s, f_s, x_s, m_s, a_s, w_s, h_s, y_s,
):
    group = pl.program_id(0)
    length = ord_ref.shape[1]
    pixels = tgt_ref.shape[2]
    entries = slots_ref.shape[1]
    per = 128 // BLOCK_GAUSSIANS

    @pl.when(group == 0)
    def _():
        gt_ref[...] = jnp.zeros_like(gt_ref)

    lane_part = lax.broadcasted_iota(jnp.int32, (ROWS, 128), 1) // BLOCK_GAUSSIANS
    lane_ids = lax.broadcasted_iota(jnp.int32, (length, length), 1)
    tile0 = first_ref[0] + group * GROUP

    def centre(t):
        tile = tile0 + t
        cx = (lax.rem(tile, TX) * TILE + TILE // 2).astype(jnp.float32)
        cy = (lax.div(tile, TX) * TILE + TILE // 2).astype(jnp.float32)
        return cx, cy

    for t in range(GROUP):
        cols = []
        for v in range(entries // per):
            chunk = None
            for b in range(per):
                block = tab_ref[slots_ref[group * GROUP + t, v * per + b]]
                chunk = block if chunk is None else jnp.where(lane_part == b, block, chunk)
            cols.append(chunk)
        fields = jnp.concatenate(cols, axis=1)
        cx, cy = centre(t)
        u = fields[0:1] - cx
        w = fields[1:2] - cy
        con_a, con_b, con_c, logo = fields[2:3], fields[3:4], fields[4:5], fields[5:6]
        f_s[t] = fields
        coefs = jnp.concatenate(
            [
                logo - 0.5 * (con_a * u * u + con_c * w * w) - con_b * u * w,
                con_a * u + con_b * w,
                con_c * w + con_b * u,
                -0.5 * con_a,
                -con_b,
                -0.5 * con_c,
                fields[6:9],
                jnp.zeros((ROWS - FIELDS, length), jnp.float32),
            ],
            axis=0,
        )
        parts = jnp.concatenate(
            list(pieces3(coefs)) + [jnp.zeros((128 - 3 * ROWS, length), jnp.float32)], axis=0
        ).astype(jnp.bfloat16)
        perm = jnp.where(ord_ref[0, :, t : t + 1] == lane_ids, 1.0, 0.0).astype(jnp.bfloat16)
        p_s[t] = perm
        x_s[pl.ds(t, length, stride=GROUP), :] = lax.dot_general(
            perm, parts, NT_DIMS, preferred_element_type=jnp.float32
        )

    rows = 64 * GROUP
    steps = length * GROUP // rows

    @pl.loop(0, steps)
    def _(c):
        part = pl.ds(pl.multiple_of(c * rows, rows), rows)
        m_s[part, :] = jnp.dot(
            x_s[part, :].astype(jnp.bfloat16), wmat_ref[...], preferred_element_type=jnp.float32
        )

    unroll = 16
    chunk = unroll * GROUP

    def twice(x):
        return jnp.concatenate([x] * (pixels // 128), axis=1)

    def load_colors(view, r):
        return [twice(view[r, pixels + 128 * ch : pixels + 128 * (ch + 1)]) for ch in range(3)]

    def views_at(c):
        part = pl.ds(pl.multiple_of(c * chunk, chunk), chunk)
        return [ref.at[part, :] for ref in (m_s, a_s, w_s, h_s)]

    def forward(c, carry):
        trans, acc = carry
        m_v, a_v, w_v, _ = views_at(c)
        for j in range(unroll):
            r = slice(j * GROUP, (j + 1) * GROUP)
            alpha = jnp.exp(m_v[r, 0:pixels])
            weight = alpha * trans
            a_v[r, :] = alpha
            w_v[r, :] = weight
            acc = tuple(a + col * weight for a, col in zip(acc, load_colors(m_v, r)))
            trans = trans - weight
        return (trans, acc)

    zero = jnp.zeros((GROUP, pixels), jnp.float32)
    trips = length // unroll
    _, image = lax.fori_loop(0, trips, forward, (zero + 1.0, (zero, zero, zero)))
    glist = []
    for ch in range(3):
        img_ref[ch] = image[ch]
        glist.append((image[ch] - tgt_ref[ch]) * (1.0 / pixels))

    def backward(i, behind):
        m_v, a_v, w_v, h_v = views_at(trips - 1 - i)
        for j in reversed(range(unroll)):
            r = slice(j * GROUP, (j + 1) * GROUP)
            c = load_colors(m_v, r)
            delta = (c[0] * glist[0] + c[1] * glist[1] + c[2] * glist[2]) - behind
            h_v[r, :] = w_v[r, :] * delta
            behind = behind + a_v[r, :] * delta
        return behind

    lax.fori_loop(0, trips, backward, zero)

    grows = jnp.concatenate(
        [jnp.zeros((16, pixels), jnp.float32)]
        + glist
        + [jnp.zeros((128 - 16 - 3 * GROUP, pixels), jnp.float32)],
        axis=0,
    )
    ghigh = grows.astype(jnp.bfloat16)
    glow = (grows - ghigh.astype(jnp.float32)).astype(jnp.bfloat16)
    gboth = jnp.concatenate([ghigh, glow], axis=0)

    def nt(a, b):
        return lax.dot_general(a, b, NT_DIMS, preferred_element_type=jnp.float32)

    @pl.loop(0, steps)
    def _(c):
        part = pl.ds(pl.multiple_of(c * rows, rows), rows)
        h = h_s[part, :]
        weight = w_s[part, :]
        h1 = h.astype(jnp.bfloat16)
        h2 = (h - h1.astype(jnp.float32)).astype(jnp.bfloat16)
        w1 = weight.astype(jnp.bfloat16)
        w2 = (weight - w1.astype(jnp.float32)).astype(jnp.bfloat16)
        bas = bas_ref[...]
        both = nt(w1, gboth)
        y_s[part, :] = (
            nt(h1, bas) + nt(h2, bas) + nt(w2, ghigh) + both[:, 0:128] + both[:, 128:256]
        )

    used = 16 + 3 * GROUP
    for t in range(GROUP):
        moments = y_s[pl.ds(t, length, stride=GROUP), :].T[0:used]
        stacked = jnp.concatenate(
            list(pieces3(moments)) + [jnp.zeros((128 - 3 * used, length), jnp.float32)], axis=0
        ).astype(jnp.bfloat16)
        back = jnp.dot(stacked, p_s[t], preferred_element_type=jnp.float32)
        back = back[0:used] + back[used : 2 * used] + back[2 * used : 3 * used]
        fields = f_s[t]
        cx, cy = centre(t)
        u = fields[0:1] - cx
        w = fields[1:2] - cy
        con_a, con_b, con_c = fields[2:3], fields[3:4], fields[4:5]
        h0, hx, hy, hxx, hxy, hyy = [back[j : j + 1] for j in range(6)]
        sx = hx - u * h0
        sy = hy - w * h0
        sxx = hxx - 2.0 * u * hx + u * u * h0
        syy = hyy - 2.0 * w * hy + w * w * h0
        sxy = hxy - u * hy - w * hx + u * w * h0
        out = jnp.concatenate(
            [
                con_a * sx + con_b * sy,
                con_c * sy + con_b * sx,
                -0.5 * sxx,
                -sxy,
                -0.5 * syy,
                h0,
            ]
            + [back[16 + ch * GROUP + t : 17 + ch * GROUP + t] for ch in range(3)]
            + [jnp.zeros((ROWS - FIELDS, length), jnp.float32)],
            axis=0,
        )
        for e in range(entries):
            slot = slots_ref[group * GROUP + t, e]
            v, b = divmod(e, per)
            gt_ref[slot] += jnp.where(lane_part == b, out[:, v * 128 : (v + 1) * 128], 0.0)


def composite(table, slots, order, goal, first_tile):
    tiles, length = order.shape
    pixels = goal.shape[-1]
    groups = tiles // GROUP
    table_rows = table.shape[0]
    order_cols = jnp.transpose(order.reshape(groups, GROUP, length), (0, 2, 1))
    basis = basis_rows(pixels)
    wmat = np.zeros((128, pixels + 3 * 128), np.float32)
    for piece in range(3):
        wmat[piece * ROWS : piece * ROWS + 6, :pixels] = basis
        for ch in range(3):
            wmat[piece * ROWS + 6 + ch, pixels + 128 * ch : pixels + 128 * (ch + 1)] = 1.0
    bas = np.zeros((128, pixels), np.float32)
    bas[:6] = basis
    full = lambda g, *_: (0, 0)
    whole = lambda g, *_: (0, 0, 0)
    image, gtab = pl.pallas_call(
        composite_kernel,
        out_shape=(
            jax.ShapeDtypeStruct((3, tiles, pixels), jnp.float32),
            jax.ShapeDtypeStruct((table_rows, ROWS, 128), jnp.float32),
        ),
        grid_spec=pltpu.PrefetchScalarGridSpec(
            num_scalar_prefetch=2,
            grid=(groups,),
            in_specs=[
                pl.BlockSpec((table_rows, ROWS, 128), whole),
                pl.BlockSpec((1, length, GROUP), lambda g, *_: (g, 0, 0)),
                pl.BlockSpec((3, GROUP, pixels), lambda g, *_: (0, g, 0)),
                pl.BlockSpec(wmat.shape, full),
                pl.BlockSpec(bas.shape, full),
            ],
            out_specs=(
                pl.BlockSpec((3, GROUP, pixels), lambda g, *_: (0, g, 0)),
                pl.BlockSpec((table_rows, ROWS, 128), whole),
            ),
            scratch_shapes=[
                pltpu.VMEM((GROUP, length, length), jnp.bfloat16),
                pltpu.VMEM((GROUP, ROWS, length), jnp.float32),
                pltpu.VMEM((length * GROUP, 128), jnp.float32),
                pltpu.VMEM((length * GROUP, pixels + 3 * 128), jnp.float32),
                pltpu.VMEM((length * GROUP, pixels), jnp.float32),
                pltpu.VMEM((length * GROUP, pixels), jnp.float32),
                pltpu.VMEM((length * GROUP, pixels), jnp.float32),
                pltpu.VMEM((length * GROUP, 128), jnp.float32),
            ],
        ),
        compiler_params=pltpu.CompilerParams(
            dimension_semantics=("arbitrary",), vmem_limit_bytes=60 * 1024 * 1024
        ),
    )(
        slots,
        first_tile,
        table,
        order_cols,
        jnp.transpose(goal, (1, 0, 2)),
        jnp.asarray(wmat, jnp.bfloat16),
        jnp.asarray(bas, jnp.bfloat16),
    )
    return jnp.transpose(image, (1, 0, 2)), gtab


SUB = 8


def project_kernel(params_ref, cam_ref, out_ref):
    @pl.loop(0, params_ref.shape[1] // SUB)
    def _(r):
        part = pl.ds(pl.multiple_of(r * SUB, SUB), SUB)
        gauss = [params_ref[i, part, :] for i in range(params_ref.shape[0])]
        camera = [cam_ref[i : i + 1, :] for i in range(cam_ref.shape[0])]
        for f, value in enumerate(project(gauss, camera)):
            out_ref[f, part, :] = value


def pullback_kernel(params_ref, grads_ref, out_ref):
    views = grads_ref.shape[0]
    depth = params_ref.shape[1]
    cam_base = FIELDS * depth

    @pl.loop(0, depth // SUB)
    def _(r):
        part = pl.ds(pl.multiple_of(r * SUB, SUB), SUB)
        gauss = [params_ref[i, part, :] for i in range(params_ref.shape[0])]

        def every_view(values):
            out = []
            for v in range(views):
                camera = [grads_ref[v, i : i + 1, :] for i in range(cam_base, grads_ref.shape[1])]
                out.append(project(values, camera))
            return out

        _, pullback = jax.vjp(every_view, gauss)
        cotangents = [
            [
                grads_ref[v, pl.ds(pl.multiple_of(f * depth + r * SUB, SUB), SUB), :]
                for f in range(FIELDS)
            ]
            for v in range(views)
        ]
        for i, value in enumerate(pullback(cotangents)[0]):
            out_ref[i, part, :] = value


def exchange_kernel(views, mine_ref, out_ref, local_sem, send_sem, recv_sem):
    me = lax.axis_index("view")
    barrier = pltpu.get_barrier_semaphore()
    right, left = lax.rem(me + 1, views), lax.rem(me + views - 1, views)
    half = mine_ref.shape[0] // 2
    parts = [pl.ds(0, half), pl.ds(half, mine_ref.shape[0] - half)]

    def signal(peer):
        pl.semaphore_signal(
            barrier, inc=1, device_id={"view": peer}, device_id_type=pl.DeviceIdType.MESH
        )

    def send(src, owner, part, peer, index):
        copy = pltpu.make_async_remote_copy(
            src_ref=src.at[parts[part]],
            dst_ref=out_ref.at[owner, parts[part]],
            send_sem=send_sem.at[index],
            recv_sem=recv_sem.at[index],
            device_id={"view": peer},
            device_id_type=pl.DeviceIdType.MESH,
        )
        copy.start()
        return copy

    if views == 4:
        signal(right)
        signal(left)
        pl.semaphore_wait(barrier, 2)
        first = send(mine_ref, me, 0, right, 0)
        second = send(mine_ref, me, 1, left, 1)
        copies = [first, second, send(mine_ref, me, 1, right, 2), send(mine_ref, me, 0, left, 3)]
        own = pltpu.make_async_copy(mine_ref, out_ref.at[me], local_sem)
        own.start()
        first.wait_recv()
        copies.append(send(out_ref.at[left], left, 0, right, 4))
        second.wait_recv()
        copies.append(send(out_ref.at[right], right, 1, left, 5))
        first.wait_send()
        second.wait_send()
        for copy in copies[2:]:
            copy.wait()
        own.wait()
        return
    peers = [lax.rem(me + step, views) for step in range(1, views)]
    for peer in peers:
        signal(peer)
    pl.semaphore_wait(barrier, views - 1)
    copies = []
    for step, peer in enumerate(peers):
        copies.append(send(mine_ref, me, 0, peer, 2 * step))
        copies.append(send(mine_ref, me, 1, peer, 2 * step + 1))
    own = pltpu.make_async_copy(mine_ref, out_ref.at[me], local_sem)
    own.start()
    own.wait()
    for copy in copies:
        copy.wait()


def exchange_views(mine):
    views = lax.axis_size("view")
    return pl.pallas_call(
        lambda *refs: exchange_kernel(views, *refs),
        out_shape=jax.ShapeDtypeStruct((views,) + mine.shape, jnp.float32),
        in_specs=[pl.BlockSpec(memory_space=pl.ANY)],
        out_specs=pl.BlockSpec(memory_space=pl.ANY),
        scratch_shapes=[
            pltpu.SemaphoreType.DMA,
            pltpu.SemaphoreType.DMA((2 * views - 2,)),
            pltpu.SemaphoreType.DMA((2 * views - 2,)),
        ],
        compiler_params=pltpu.CompilerParams(collective_id=0, has_side_effects=True),
        name="exchange_views",
    )(mine)


def swap_kernel(cells, mine_ref, out_ref, local_sem, send_sem, recv_sem):
    me = lax.axis_index("cell")
    barrier = pltpu.get_barrier_semaphore()
    peers = [lax.rem(me + step, cells) for step in range(1, cells)]
    for peer in peers:
        pl.semaphore_signal(
            barrier, inc=1, device_id={"cell": peer}, device_id_type=pl.DeviceIdType.MESH
        )
    pl.semaphore_wait(barrier, cells - 1)
    copies = [
        pltpu.make_async_remote_copy(
            src_ref=mine_ref.at[peer],
            dst_ref=out_ref.at[me],
            send_sem=send_sem.at[step],
            recv_sem=recv_sem.at[step],
            device_id={"cell": peer},
            device_id_type=pl.DeviceIdType.MESH,
        )
        for step, peer in enumerate(peers)
    ]
    for copy in copies:
        copy.start()
    own = pltpu.make_async_copy(mine_ref.at[me], out_ref.at[me], local_sem)
    own.start()
    own.wait()
    for copy in copies:
        copy.wait()


def swap_cells(mine, collective_id):
    cells = lax.axis_size("cell")
    blocks = mine.reshape(cells, -1, 128)
    out = pl.pallas_call(
        lambda *refs: swap_kernel(cells, *refs),
        out_shape=jax.ShapeDtypeStruct(blocks.shape, jnp.float32),
        in_specs=[pl.BlockSpec(memory_space=pl.ANY)],
        out_specs=pl.BlockSpec(memory_space=pl.ANY),
        scratch_shapes=[
            pltpu.SemaphoreType.DMA,
            pltpu.SemaphoreType.DMA((cells - 1,)),
            pltpu.SemaphoreType.DMA((cells - 1,)),
        ],
        compiler_params=pltpu.CompilerParams(collective_id=collective_id, has_side_effects=True),
        name=f"swap_cells_{collective_id}",
    )(blocks)
    return out.reshape(mine.shape)


def local(params, camera, targets, send_blocks, tile_blocks, tile_order):
    cells = lax.axis_size("cell")
    cell_index = lax.axis_index("cell")
    values_n, owned = params.shape
    owned_blocks = owned // BLOCK_GAUSSIANS
    per_peer = send_blocks.shape[3]
    slots_n = cells * per_peer
    block_values = FIELDS * BLOCK_GAUSSIANS
    picks = send_blocks[0, 0].reshape(-1)
    depth = owned // 128
    spread = params.reshape(values_n, depth, 128)
    cam_rows = jnp.broadcast_to(
        jnp.pad(camera[0], (0, -camera.shape[1] % SUB))[:, None],
        (camera.shape[1] + -camera.shape[1] % SUB, 128),
    )
    fields = pl.pallas_call(
        project_kernel,
        out_shape=jax.ShapeDtypeStruct((FIELDS, depth, 128), jnp.float32),
        name="project",
    )(spread, cam_rows)
    by_block = jnp.transpose(
        fields.reshape(FIELDS, owned_blocks, BLOCK_GAUSSIANS), (1, 0, 2)
    ).reshape(owned_blocks, block_values)
    chosen = jnp.take(by_block, picks, axis=0).reshape(cells, per_peer * block_values)
    received = swap_cells(chosen, 1)
    received = received.reshape(slots_n, FIELDS, BLOCK_GAUSSIANS)
    dummy = np.zeros((1, FIELDS, BLOCK_GAUSSIANS), np.float32)
    dummy[:, 5] = -1e30
    table = jnp.concatenate([received, jnp.asarray(dummy)], axis=0)
    table = jnp.tile(
        jnp.pad(table, ((0, 0), (0, ROWS - FIELDS), (0, 0))), (1, 1, 128 // BLOCK_GAUSSIANS)
    )
    blocks = tile_blocks[0]
    slots = jnp.where(blocks < 0, slots_n, blocks)
    first_tile = (cell_index * blocks.shape[0]).astype(jnp.int32).reshape(1)
    picture, gtab = composite(table, slots, tile_order[0], targets[0], first_tile)
    slot_grad = (
        gtab[:slots_n, :FIELDS]
        .reshape(slots_n, FIELDS, 128 // BLOCK_GAUSSIANS, BLOCK_GAUSSIANS)
        .sum(2)
        .reshape(cells, per_peer * block_values)
    )
    returned = swap_cells(slot_grad, 2)
    chosen_of = (jnp.arange(owned_blocks)[:, None] == picks[None, :]).astype(jnp.float32)
    summed = jnp.dot(
        chosen_of, returned.reshape(slots_n, block_values), precision=HIGHEST_PRECISE
    )
    summed = jnp.transpose(
        summed.reshape(owned_blocks, FIELDS, BLOCK_GAUSSIANS), (1, 0, 2)
    ).reshape(FIELDS * depth, 128)
    by_view = exchange_views(jnp.concatenate([summed, cam_rows], axis=0))
    total = pl.pallas_call(
        pullback_kernel,
        out_shape=jax.ShapeDtypeStruct((values_n, depth, 128), jnp.float32),
        name="pullback",
    )(spread, by_view)
    return (picture[None], total.reshape(values_n, owned))


def solution(mesh):
    return jax.shard_map(
        local,
        mesh=mesh,
        in_specs=(
            P(None, "cell"),
            P("view", None),
            P("view", "cell", None, None),
            P("view", "cell", None, None),
            P("view", "cell", None),
            P("view", "cell", None),
        ),
        out_specs=(P("view", "cell", None, None), P(None, "cell")),
        check_vma=False,
    )
```
